128 devices in a mesh: latent: 16 (over z, y), row: 2 (over x_hi), col: 4 (over x_lo, core).
Axes of the slice: x: 4 (x_hi: 2, x_lo: 2; x = x_hi * 2 + x_lo), y: 4, z: 4, core: 2. Of those that a mesh axis runs over, the one named last changes fastest.
Arguments:
- observations: bfloat16 [128, 64, 2048], P('col', 'latent', 'row'), may hold values from -6 to 6
- rotation: float32 [64, 16], replicated, may hold values from -0.75 to 0.75
- ordering: int32 [2048], P('row'), may hold values from 0 to 2047, as said below
- working: bfloat16 [16, 2048, 2048], P('latent', 'row', 'col'), as said below
- factor_inverse: bfloat16 [16, 2, 512, 512], P('latent'), as said below
- panel_index: int32 [2], replicated, may hold values from 0 to 3
Outputs:
- trailing: float32 [16, 2048, 2048], P('latent', 'row', 'col')
- panels: bfloat16 [16, 2, 2048, 512], P('latent', None, 'row', 'col')
- whitened: float32 [16, 128, 2048], P('latent', 'col', 'row')
The draws below stay inside these ranges and needn't reach their ends.
Inputs may be any that keep to these rules, and one draw needn't show every extreme that they name: `ordering`: a permutation of the stations that maps each block of 1024 consecutive positions onto the same block. `working`: symmetric in its last two dimensions. `factor_inverse`: lower triangular in its last two dimensions, with a positive diagonal.
All inputs are finite; a program needn't handle non-finite values.
Results may differ from the reference program's by a relative error of at most 0.0047.
Values may be sent and summed in bfloat16 or wider, within the bound.
A program may use at most 64 MiB of HBM per device.

```python
import jax
import jax.numpy as jnp
from jax import lax

VARS = 64
NB = 512
PANELS = 2
STATIONS = 2048
LATENTS = 16
TIMES = 128
N_ROW = 2


def draw_ordering(key, part):
    block = STATIONS // N_ROW
    keys = jax.random.split(key, N_ROW)
    shuffled = jax.vmap(lambda single: jax.random.permutation(single, block))(keys)
    offsets = (jnp.arange(N_ROW, dtype=jnp.int32) * block)[:, None]
    return (shuffled.astype(jnp.int32) + offsets).reshape(STATIONS)


def draw_working(key, part):

    def one_latent(index):
        single = jax.random.fold_in(jax.random.fold_in(key, 71), index)
        raw = jax.random.normal(jax.random.fold_in(single, 1), (STATIONS, STATIONS), jnp.float32)
        symmetric = 0.5 * (raw + raw.T)
        diag_add = jax.random.uniform(jax.random.fold_in(single, 2), (STATIONS,), jnp.float32, 1.0, 3.0)
        places = jnp.arange(STATIONS)
        symmetric = symmetric + jnp.where(places[:, None] == places[None, :], diag_add[None, :], 0.0)
        return symmetric.astype(jnp.bfloat16)
    return lax.map(one_latent, jnp.arange(LATENTS))


def draw_factor_inverse(key, part):
    shape = (LATENTS, PANELS, NB, NB)
    diag_vals = jax.random.uniform(jax.random.fold_in(key, 11), shape, jnp.float32, 0.06, 0.18)
    lower_vals = jax.random.normal(jax.random.fold_in(key, 12), shape, jnp.float32) * (0.1 / NB ** 0.5)
    rows_at = jnp.arange(NB)[:, None]
    cols_at = jnp.arange(NB)[None, :]
    result = jnp.where(rows_at == cols_at, diag_vals, jnp.where(cols_at < rows_at, lower_vals, 0.0))
    return result.astype(jnp.bfloat16)


def shard_levels(rng, shape, cuts, least, top_value):
    loudness = 1.0
    for dim, blocks in cuts:
        steps = jax.random.uniform(jax.random.fold_in(jax.random.fold_in(rng, 6), dim), (blocks,), jnp.float32, least / len(cuts), top_value / len(cuts))
        loudness = loudness * jnp.repeat(jnp.exp(steps), shape[dim] // blocks).reshape((-1,) + (1,) * (len(shape) - 1 - dim))
    return loudness


def bell_draw(own_key, extent, scale, limit, pieces=(), kind=jnp.bfloat16):
    loudness = shard_levels(own_key, extent, pieces, -0.22, 0.18) if pieces else 1.0
    values = jax.random.normal(own_key, extent, jnp.float32) * scale * loudness
    return jnp.minimum(jnp.maximum(values, -limit), limit).astype(kind)


def setup_inputs(seed: int = 0) -> dict:
    splits = jax.random.split(jax.random.key(seed), 7)
    return {
        "observations": bell_draw(splits[0], (TIMES, VARS, STATIONS), 1.0, 6.0, ((0, 4), (1, 16), (2, 2))),
        "rotation": bell_draw(splits[1], (VARS, LATENTS), VARS ** -0.5, 0.75, (), jnp.float32),
        "ordering": draw_ordering(jax.random.fold_in(splits[6], 71), 0),
        "working": draw_working(jax.random.fold_in(splits[6], 71), 0),
        "factor_inverse": draw_factor_inverse(jax.random.fold_in(splits[6], 71), 0),
        "panel_index": jax.random.randint(splits[5], (PANELS,), 0, STATIONS // NB).astype(jnp.int32),
    }


def reference(observations, rotation, ordering, working, factor_inverse, panel_index):
    rotated = jnp.einsum("tvs,vl->lts", observations.astype(jnp.float32), rotation, precision=lax.Precision.HIGHEST)
    fields = jnp.take(rotated, ordering, axis=2)

    def one_latent(packed):
        tile, inverses, field = packed
        matrix = tile.astype(jnp.float32)
        factors = []
        for panel in range(PANELS):
            inverse = inverses[panel].astype(jnp.float32)
            start = (panel_index[panel] * NB).astype(jnp.int32)
            column_block = lax.dynamic_slice_in_dim(matrix, start, NB, 1).astype(jnp.bfloat16).astype(jnp.float32)
            factor = jnp.dot(column_block, inverse.T, precision=lax.Precision.HIGHEST).astype(jnp.bfloat16)
            rhs_part = lax.dynamic_slice_in_dim(field, start, NB, 1)
            solved = jnp.dot(rhs_part, inverse.T, precision=lax.Precision.HIGHEST).astype(jnp.bfloat16)
            wide_factor = factor.astype(jnp.float32)
            matrix = matrix - jnp.dot(wide_factor, wide_factor.T, precision=lax.Precision.HIGHEST)
            field = field - jnp.dot(solved.astype(jnp.float32), wide_factor.T, precision=lax.Precision.HIGHEST)
            factors.append(factor)
        return matrix, jnp.stack(factors), field

    trailing, panels, whitened = lax.map(one_latent, (working, factor_inverse, fields))
    return (trailing, panels, whitened)
```

```python
import functools

import jax
import jax.numpy as jnp
from jax import lax
from jax.experimental import pallas as pl
from jax.experimental.pallas import tpu as pltpu
from jax.sharding import PartitionSpec as P

MESH = pl.DeviceIdType.MESH
F32 = jnp.float32
BF16 = jnp.bfloat16
NB = 512
HALF = 1024
CHUNKS = 4
CH = HALF // CHUNKS
PER_QUARTER = CHUNKS // 2


def nt(a, b):
    return lax.dot_general(a, b, (((1,), (1,)), ((), ())), preferred_element_type=F32)


def nn(a, b):
    return jnp.dot(a, b, preferred_element_type=F32)


def split(value):
    high = value.astype(BF16)
    return high, (value - high.astype(F32)).astype(BF16)


def kernel(
    pair, lat,
    obs, rot, order, w_hbm, inv_hbm,
    trail, pans, white,
    inv, w, brow, bc, g, gt, f0, f1, fc, fk, x, xf, y, z, zf, pm, field, solved,
    send, rsem, bsem, gsem, tsem, vsem, lsem, s1, r1, s2, r2,
):
    halves = [k // 2 for k in pair]
    cores = [k % 2 for k in pair]
    distinct = (0,) if pair[0] == pair[1] else (0, 1)
    slot = (0, distinct[-1])
    lid = lax.axis_index("latent")
    r = lax.axis_index("row")
    c = lax.axis_index("col")
    xl = c // 2
    core = c % 2
    steps = obs.shape[0] // lat
    local_vars = obs.shape[1]
    pending = []
    count = [0]

    def push(cond, src, dst, recv, row, col):
        sem = send.at[count[0]]
        count[0] += 1

        def make():
            return pltpu.make_async_remote_copy(
                src_ref=src, dst_ref=dst, send_sem=sem, recv_sem=recv,
                device_id={"row": row, "col": col}, device_id_type=MESH,
            )

        @pl.when(cond)
        def _():
            make().start()

        pending.append((cond, make))

    def arrived(ref, sem):
        pltpu.make_async_copy(ref, ref, sem).wait()

    def rows(ref, m):
        return ref.at[pl.ds(m * CH, CH), :]

    load_inv = pltpu.make_async_copy(inv_hbm.at[0], inv, lsem.at[0])
    load_w = pltpu.make_async_copy(w_hbm.at[0], w, lsem.at[1])
    load_inv.start()
    load_w.start()
    own_x = pltpu.make_async_copy(obs.at[pl.ds(lid * steps, steps)], x.at[lid], lsem.at[2])
    own_x.start()

    barrier = pltpu.get_barrier_semaphore()

    def greet(d, carry):
        pl.semaphore_signal(
            barrier, inc=1, device_id={"latent": lax.rem(lid + d, lat)}, device_id_type=MESH
        )
        return carry

    lax.fori_loop(1, lat, greet, 0)

    def greet_group(d, carry):
        other = lax.rem(r * 4 + c + d, 8)
        pl.semaphore_signal(
            barrier, inc=1, device_id={"row": other // 4, "col": other % 4}, device_id_type=MESH
        )
        return carry

    lax.fori_loop(1, 8, greet_group, 0)
    pl.semaphore_wait(barrier, lat - 1 + 7)

    for m in range(CHUNKS):
        for p in distinct:
            h, j = halves[p], cores[p]
            holder = (xl == h) & (core == j)
            src = rows(w_hbm.at[0], m)
            quarter = m // PER_QUARTER
            push(holder, src, rows(brow.at[p], m), rsem.at[p, m], r, 2 * (1 - h) + quarter)
            push(holder, src, rows(brow.at[p], m), rsem.at[p, m], r, 2 * h + 1 - j)

            @pl.when(holder)
            def _():
                pltpu.make_async_copy(src, rows(brow.at[p], m), rsem.at[p, m]).start()

    h0, h1 = halves
    j0, j1 = cores
    same = h0 == h1
    is_s = (r == h0) & (xl == h0)
    is_n = (r == h0) & (xl == 1 - h0)
    is_d = (r == 1 - h0) & (xl == h0)
    is_t = (r == 1 - h0) & (xl == 1 - h0)
    if same:
        for i in range(2):
            for m in range(PER_QUARTER):
                push(
                    is_s & (core == j0), rows(w_hbm.at[0], j1 * PER_QUARTER + m), rows(g, m),
                    gsem.at[m], 1 - h0, 2 * (1 - h0) + i,
                )
    else:
        push(
            is_n & (core == j1), w_hbm.at[0, pl.ds(j0 * NB, NB), :], gt, tsem,
            h0, 2 * (1 - h0) + 1 - j1,
        )

    def first(d):
        to = lax.rem(lid + d, lat)
        return pltpu.make_async_remote_copy(
            src_ref=obs.at[pl.ds(to * steps, steps)], dst_ref=x.at[lid],
            send_sem=s1.at[d], recv_sem=r1.at[d],
            device_id={"latent": to}, device_id_type=MESH,
        )

    def second(d):
        to = lax.rem(lid + d, lat)
        return pltpu.make_async_remote_copy(
            src_ref=y.at[to], dst_ref=z.at[lid],
            send_sem=s2.at[d], recv_sem=r2.at[d],
            device_id={"latent": to}, device_id_type=MESH,
        )

    def each(action):
        def step(d, carry):
            action(d)
            return carry

        lax.fori_loop(1, lat, step, 0)

    each(lambda d: first(d).start())

    place = order[...] - r * HALF
    for i in range(HALF // 128):
        at = lax.broadcasted_iota(jnp.int32, (128, HALF), 0) + i * 128
        pm[pl.ds(i * 128, 128), :] = jnp.where(at == place, 1.0, 0.0).astype(BF16)

    mixed_rows = lat * steps
    depth = lat * steps * local_vars
    total_vars = lat * local_vars
    pick_latent = (
        lax.broadcasted_iota(jnp.int32, (mixed_rows, lat), 0) // steps
        == lax.broadcasted_iota(jnp.int32, (mixed_rows, lat), 1)
    )
    pick_latent = jnp.where(pick_latent, 1.0, 0.0).astype(BF16)
    along = lax.broadcasted_iota(jnp.int32, (total_vars, depth), 1)
    pick_var = (along // (steps * local_vars)) * local_vars + along % local_vars
    pick_var = pick_var == lax.broadcasted_iota(jnp.int32, (total_vars, depth), 0)
    pick_var = jnp.where(pick_var, 1.0, 0.0).astype(BF16)
    wide = lax.broadcasted_iota(jnp.int32, (mixed_rows, depth), 1)
    tall = lax.broadcasted_iota(jnp.int32, (mixed_rows, depth), 0)
    same_step = (wide // local_vars) % steps == tall % steps

    def mixer(part):
        spread = nn(nt(pick_latent, part).astype(BF16), pick_var)
        return jnp.where(same_step, spread, 0.0).astype(BF16)

    rot_high, rot_low = split(rot[...])
    mix_high, mix_low = mixer(rot_high), mixer(rot_low)

    load_inv.wait()
    load_w.wait()

    def relay(m):
        for p in distinct:
            h = halves[p]
            quarter = m // PER_QUARTER
            block = rows(brow.at[p], m)
            arrived(block, rsem.at[p, m])
            passer = (xl == 1 - h) & (core == quarter)
            push(passer, block, block, rsem.at[p, m], r, 2 * (1 - h) + 1 - quarter)
            inner = m - quarter * PER_QUARTER
            push(
                passer & (r == h), block, rows(bc.at[p], inner), bsem.at[p, inner],
                1 - h, 2 * h + quarter,
            )
            if p == 0 and not same and quarter == j1:
                push(
                    is_t & (core == j1), block, rows(g, inner), gsem.at[inner], h0, 2 * h0 + j1
                )
        f0[pl.ds(m * CH, CH), :] = nt(brow[0, pl.ds(m * CH, CH), :], inv[0]).astype(BF16)

    relay(0)
    own_x.wait()
    each(lambda d: first(d).wait_recv())
    for i in range(lat):
        for t in range(steps):
            xf[pl.ds((i * steps + t) * local_vars, local_vars), :] = x[i, t].astype(F32)
    samples = xf[...].astype(BF16)
    mixed = nn(mix_high, samples) + nn(mix_low, samples)
    for i in range(lat):
        y[i] = mixed[i * steps : (i + 1) * steps]
    each(lambda d: second(d).start())
    own_z = pltpu.make_async_copy(y.at[lid], z.at[lid], lsem.at[3])
    own_z.start()
    relay(1)
    relay(2)
    own_z.wait()
    each(lambda d: second(d).wait_recv())
    for i in range(lat):
        zf[pl.ds(i * steps, steps), :] = z[i]
    high, low = split(zf[...])
    field[...] = nn(high, pm[...]) + nn(low, pm[...])

    def solve(p):
        part = field[:, pl.ds(cores[p] * NB, NB)]
        if p == 1:
            part = part - nt(solved[0], fk[...])
        top, rest = split(part)
        solved[p] = (nt(top, inv[p]) + nt(rest, inv[p])).astype(BF16)

    def share(p):
        owner = r == halves[p]

        @pl.when(owner)
        def _():
            solve(p)

        push(owner, solved.at[p], solved.at[p], vsem.at[p], 1 - halves[p], c)

        @pl.when(r != halves[p])
        def _():
            arrived(solved.at[p], vsem.at[p])

    relay(3)

    for p in distinct:
        @pl.when(r == xl)
        def _():
            bc[p] = brow[p, pl.ds(pl.multiple_of(core * NB, NB), NB), :]

        @pl.when((r == halves[p]) & (xl == 1 - halves[p]))
        def _():
            bc[p] = w[pl.ds(cores[p] * NB, NB), :].T

        @pl.when((r == 1 - halves[p]) & (xl == halves[p]))
        def _():
            for m in range(PER_QUARTER):
                arrived(rows(bc.at[p], m), bsem.at[p, m])

    quarter_rows = pl.ds(j1 * NB, NB)
    if same:
        for m in range(PER_QUARTER):
            push(
                is_d & (core == j1), rows(bc.at[0], m), rows(g, m), gsem.at[m],
                1 - h0, 2 * h0 + 1 - j1,
            )

        @pl.when(r == h0)
        def _():
            g[...] = brow[0, quarter_rows, :]

        @pl.when(is_d & (core == j1))
        def _():
            g[...] = bc[0]

        @pl.when(is_t | (is_d & (core == 1 - j1)))
        def _():
            for m in range(PER_QUARTER):
                arrived(rows(g, m), gsem.at[m])
    else:
        @pl.when(r == 1 - h0)
        def _():
            g[...] = brow[0, quarter_rows, :]

        @pl.when(is_n & (core == j1))
        def _():
            g[...] = bc[0]

        @pl.when(is_n & (core == 1 - j1))
        def _():
            arrived(gt, tsem)
            g[...] = gt[...].T

        for m in range(PER_QUARTER):
            @pl.when(is_s)
            def _():
                arrived(rows(g, m), gsem.at[m])

            push(
                is_s & (core == j1), rows(g, m), rows(g, m), gsem.at[m], h0, 2 * h0 + 1 - j1
            )

    fk[...] = nt(g[...], inv[0]).astype(BF16)
    share(0)
    share(1)
    fc[0] = nt(bc[0], inv[0]).astype(BF16)
    below = (bc[slot[1]].astype(F32) - nt(fc[0], fk[...])).astype(BF16)
    fc[1] = nt(below, inv[1]).astype(BF16)

    def finish(m, carry):
        span = pl.ds(pl.multiple_of(m * CH, CH), CH)
        left = f0[span, :]
        block = (brow[slot[1], span, :].astype(F32) - nt(left, fk[...])).astype(BF16)
        right = nt(block, inv[1]).astype(BF16)
        f1[span, :] = right
        trail[0, span, :] = w[span, :].astype(F32) - (nt(left, fc[0]) + nt(right, fc[1]))
        return carry

    lax.fori_loop(0, CHUNKS, finish, 0)
    mine = pl.ds(pl.multiple_of(c * 128, 128), 128)
    pans[0, 0] = f0[:, mine]
    pans[0, 1] = f1[:, mine]
    white[0] = field[...] - (nt(solved[0], f0[...]) + nt(solved[1], f1[...]))

    for cond, make in pending:
        @pl.when(cond)
        def _():
            make().wait_send()

    each(lambda d: first(d).wait_send())
    each(lambda d: second(d).wait_send())


def solution(mesh):
    lat = mesh.shape["latent"]

    def local(observations, rotation, ordering, working, factor_inverse, panel_index):
        times, local_vars, stations = observations.shape
        steps = times // lat
        vmem = pl.BlockSpec(memory_space=pltpu.VMEM)
        anyw = pl.BlockSpec(memory_space=pl.ANY)

        def call(pair, *operands):
            return pl.pallas_call(
                functools.partial(kernel, pair, lat),
                out_shape=(
                    jax.ShapeDtypeStruct((1, HALF, NB), F32),
                    jax.ShapeDtypeStruct((1, 2, HALF, 128), BF16),
                    jax.ShapeDtypeStruct((1, times, HALF), F32),
                ),
                in_specs=[anyw, vmem, vmem, anyw, anyw],
                out_specs=(vmem, vmem, vmem),
                scratch_shapes=[
                    pltpu.VMEM((2, NB, NB), BF16),
                    pltpu.VMEM((HALF, NB), BF16),
                    pltpu.VMEM((2, HALF, NB), BF16),
                    pltpu.VMEM((2, NB, NB), BF16),
                    pltpu.VMEM((NB, NB), BF16),
                    pltpu.VMEM((NB, NB), BF16),
                    pltpu.VMEM((HALF, NB), BF16),
                    pltpu.VMEM((HALF, NB), BF16),
                    pltpu.VMEM((2, NB, NB), BF16),
                    pltpu.VMEM((NB, NB), BF16),
                    pltpu.VMEM((lat, steps, local_vars, HALF), BF16),
                    pltpu.VMEM((times * local_vars, HALF), F32),
                    pltpu.VMEM((lat, steps, HALF), F32),
                    pltpu.VMEM((lat, steps, HALF), F32),
                    pltpu.VMEM((times, HALF), F32),
                    pltpu.VMEM((HALF, HALF), BF16),
                    pltpu.VMEM((times, HALF), F32),
                    pltpu.VMEM((2, times, NB), BF16),
                    pltpu.SemaphoreType.DMA((48,)),
                    pltpu.SemaphoreType.DMA((2, CHUNKS)),
                    pltpu.SemaphoreType.DMA((2, PER_QUARTER)),
                    pltpu.SemaphoreType.DMA((PER_QUARTER,)),
                    pltpu.SemaphoreType.DMA,
                    pltpu.SemaphoreType.DMA((2,)),
                    pltpu.SemaphoreType.DMA((4,)),
                    pltpu.SemaphoreType.DMA((lat,)),
                    pltpu.SemaphoreType.DMA((lat,)),
                    pltpu.SemaphoreType.DMA((lat,)),
                    pltpu.SemaphoreType.DMA((lat,)),
                ],
                compiler_params=pltpu.CompilerParams(
                    collective_id=pair[0] * 4 + pair[1], has_side_effects=True,
                    vmem_limit_bytes=48 << 20,
                ),
                name=f"panels_{pair[0]}{pair[1]}",
            )(*operands)

        branches = [functools.partial(call, (a, b)) for a in range(4) for b in range(4)]
        choice = panel_index[0] * 4 + panel_index[1]
        return lax.switch(
            choice, branches,
            observations, rotation, ordering.reshape(1, HALF), working, factor_inverse,
        )

    return jax.shard_map(
        local,
        mesh=mesh,
        in_specs=(
            P("col", "latent", "row"),
            P(),
            P("row"),
            P("latent", "row", "col"),
            P("latent", None, None, None),
            P(),
        ),
        out_specs=(
            P("latent", "row", "col"),
            P("latent", None, "row", "col"),
            P("latent", "col", "row"),
        ),
        check_vma=False,
    )
```

```python
import functools

import jax
import jax.numpy as jnp
from jax import lax
from jax.experimental import pallas as pl
from jax.experimental.pallas import tpu as pltpu
from jax.sharding import PartitionSpec as P

MESH = pl.DeviceIdType.MESH
F32 = jnp.float32
BF16 = jnp.bfloat16
NB = 512
HALF = 1024
PER = 8
CH = NB // PER
TILE = 256


def nt(a, b):
    return lax.dot_general(a, b, (((1,), (1,)), ((), ())), preferred_element_type=F32)


def nn(a, b):
    return jnp.dot(a, b, preferred_element_type=F32)


def split(value):
    high = value.astype(BF16)
    return high, (value - high.astype(F32)).astype(BF16)


def aligned(index, unit):
    return pl.ds(pl.multiple_of(index * unit, unit), unit)


def loop(start, stop, action):
    def step(i, carry):
        action(i)
        return carry

    lax.fori_loop(start, stop, step, 0)


def kernel(
    halves, lat,
    which, obs, rot_hbm, order_hbm, w_hbm, inv_hbm,
    trail, pans, white,
    inv, ww, b, bo, f, x, xf, y, z, zf, pm, field, solved, rot, order,
    lsem, swap, rsem, bsem, osem, gsem, vsem, hold, pair, down, osend, gsend, gpass, vsend,
    s1, r1, s2, r2,
):
    h0, h1 = halves
    same = h0 == h1
    lid = lax.axis_index("latent")
    r = lax.axis_index("row")
    c = lax.axis_index("col")
    xl = c // 2
    core = c % 2
    mate = 2 * xl + 1 - core
    odd = [(which[p] & 1).astype(F32) for p in range(2)]
    steps = obs.shape[0] // lat
    local_vars = obs.shape[1]
    turned = jnp.where(r == h1, 1.0, 0.0) * odd[1]

    def choose(low, high, weight):
        mix = jnp.full(low.shape, weight, F32).astype(low.dtype)
        return low * (1 - mix) + high * mix

    def remote(src, dst, send, recv, row, col):
        return pltpu.make_async_remote_copy(
            src_ref=src, dst_ref=dst, send_sem=send, recv_sem=recv,
            device_id={"row": row, "col": col}, device_id_type=MESH,
        )

    def arrived(ref, sem):
        pltpu.make_async_copy(ref, ref, sem).wait()

    def chunk(p, s, base=0):
        return b.at[p, pl.ds(pl.multiple_of(base + s * CH, CH), CH), :]

    loads = [
        pltpu.make_async_copy(w_hbm.at[0], ww.at[core], lsem.at[0]),
        pltpu.make_async_copy(inv_hbm.at[0], inv, lsem.at[1]),
        pltpu.make_async_copy(obs.at[pl.ds(lid * steps, steps)], x.at[lid], lsem.at[2]),
        pltpu.make_async_copy(rot_hbm, rot, lsem.at[3]),
        pltpu.make_async_copy(order_hbm, order, lsem.at[4]),
    ]
    for load in loads:
        load.start()

    barrier = pltpu.get_barrier_semaphore()

    def greet(d):
        pl.semaphore_signal(
            barrier, inc=1, device_id={"latent": lax.rem(lid + d, lat)}, device_id_type=MESH
        )

    def greet_group(d):
        other = lax.rem(r * 4 + c + d, 8)
        pl.semaphore_signal(
            barrier, inc=1, device_id={"row": other // 4, "col": other % 4}, device_id_type=MESH
        )

    loop(1, lat, greet)
    loop(1, 8, greet_group)
    pl.semaphore_wait(barrier, lat - 1 + 7)

    swapper = (xl == h0) | (xl == h1)

    def swapping():
        return remote(w_hbm.at[0], ww.at[core], swap.at[0], swap.at[1], r, mate)

    @pl.when(swapper)
    def _():
        swapping().start()

    def first(d):
        to = lax.rem(lid + d, lat)
        return pltpu.make_async_remote_copy(
            src_ref=obs.at[pl.ds(to * steps, steps)], dst_ref=x.at[lid],
            send_sem=s1.at[d], recv_sem=r1.at[d],
            device_id={"latent": to}, device_id_type=MESH,
        )

    def second(d):
        to = lax.rem(lid + d, lat)
        return pltpu.make_async_remote_copy(
            src_ref=y.at[to], dst_ref=z.at[lid],
            send_sem=s2.at[d], recv_sem=r2.at[d],
            device_id={"latent": to}, device_id_type=MESH,
        )

    loop(1, lat, lambda d: first(d).start())
    for load in loads:
        load.wait()

    def holding(p, t):
        s = 2 * t + core
        return remote(chunk(p, s), chunk(p, s), hold.at[p, t], rsem.at[p, s], r, 2 * (1 - xl) + core)

    def stage(p, s):
        at = aligned(s, CH)
        value = choose(ww[0, at, :], ww[1, at, :], odd[p])
        if p == 0 and not same:
            flip = aligned((s + PER) % (2 * PER), CH)
            value = choose(value, choose(ww[0, flip, :], ww[1, flip, :], odd[p]), turned)
        b[p, at, :] = value

    @pl.when(swapper)
    def _():
        arrived(ww.at[1 - core], swap.at[1])

    for p in range(2):
        @pl.when(xl == halves[p])
        def _():
            loop(0, PER, lambda t: stage(p, 2 * t + core))

    def hold_all(t):
        for p in range(2):
            @pl.when(xl == halves[p])
            def _():
                holding(p, t).start()

    loop(0, PER, hold_all)
    for p in range(2):
        @pl.when(xl == halves[p])
        def _():
            loop(0, PER, lambda t: stage(p, 2 * t + 1 - core))

    is_n = (r == h0) & (xl == 1 - h0)
    source = (r == h1) & (xl == h1)
    sink = (r == 1 - h1) & (xl == 1 - h1)
    swing = (r == 1 - h1) & (xl == h1)
    g_at = pl.ds(HALF + NB, NB)
    bc_at = pl.ds(HALF, NB)

    def across(t):
        s = 2 * t + core
        src = chunk(0, s, HALF + NB) if same else chunk(0, s)
        return remote(
            src, chunk(0, s, HALF + NB), gsend.at[t], gsem.at[s], 1 - h1, 2 * (1 - h1) + core
        )

    def pick_own():
        if same:
            b[0, g_at, :] = choose(b[0, :NB, :], b[0, NB:HALF, :], odd[1])
        else:
            b[0, g_at, :] = b[0, :NB, :]

    if same:
        @pl.when(source)
        def _():
            pick_own()
            loop(0, PER // 2, lambda t: across(t).start())

    place = order[...] - r * HALF

    def permutation(i):
        at = lax.broadcasted_iota(jnp.int32, (128, HALF), 0) + i * 128
        pm[aligned(i, 128), :] = jnp.where(at == place, 1.0, 0.0).astype(BF16)

    loop(0, HALF // 128, permutation)

    mixed_rows = lat * steps
    depth = lat * steps * local_vars
    total_vars = lat * local_vars
    pick_latent = (
        lax.broadcasted_iota(jnp.int32, (mixed_rows, lat), 0) // steps
        == lax.broadcasted_iota(jnp.int32, (mixed_rows, lat), 1)
    )
    pick_latent = jnp.where(pick_latent, 1.0, 0.0).astype(BF16)
    along = lax.broadcasted_iota(jnp.int32, (total_vars, depth), 1)
    pick_var = (along // (steps * local_vars)) * local_vars + along % local_vars
    pick_var = pick_var == lax.broadcasted_iota(jnp.int32, (total_vars, depth), 0)
    pick_var = jnp.where(pick_var, 1.0, 0.0).astype(BF16)
    wide = lax.broadcasted_iota(jnp.int32, (mixed_rows, depth), 1)
    tall = lax.broadcasted_iota(jnp.int32, (mixed_rows, depth), 0)
    same_step = (wide // local_vars) % steps == tall % steps

    def mixer(part):
        spread = nn(nn(pick_latent, part).astype(BF16), pick_var)
        return jnp.where(same_step, spread, 0.0).astype(BF16)

    rot_high, rot_low = split(rot[...])
    mix_high, mix_low = mixer(rot_high), mixer(rot_low)

    def to_mate(p, t):
        s = 2 * t + core
        return remote(chunk(p, s), chunk(p, s), pair.at[p, t], rsem.at[p, s], r, mate)

    def to_down(p, t):
        s = 2 * t + core
        return remote(
            chunk(p, s), chunk(p, s % PER, HALF), down.at[p, t], bsem.at[p, s % PER],
            1 - halves[p], 2 * halves[p] + s // PER,
        )

    def relay(t):
        s = 2 * t + core
        for p in range(2):
            @pl.when(xl == 1 - halves[p])
            def _():
                arrived(chunk(p, s), rsem.at[p, s])
                to_mate(p, t).start()

                @pl.when(r == halves[p])
                def _():
                    to_down(p, t).start()

                if p == 0 and not same:
                    @pl.when((r == h1) & (t < PER // 2))
                    def _():
                        across(t).start()

    loop(0, 2, relay)
    loop(1, lat, lambda d: first(d).wait_recv())
    for i in range(lat):
        for t in range(steps):
            xf[pl.ds((i * steps + t) * local_vars, local_vars), :] = x[i, t].astype(F32)
    samples = xf[...].astype(BF16)
    mixed = nn(mix_high, samples) + nn(mix_low, samples)
    for i in range(lat):
        y[i] = mixed[i * steps : (i + 1) * steps]
    loop(1, lat, lambda d: second(d).start())
    own_z = pltpu.make_async_copy(y.at[lid], z.at[lid], lsem.at[5])
    own_z.start()
    loop(2, 5, relay)
    own_z.wait()
    loop(1, lat, lambda d: second(d).wait_recv())
    for i in range(lat):
        zf[pl.ds(i * steps, steps), :] = z[i]
    high, low = split(zf[...])
    field[...] = nn(high, pm[...]) + nn(low, pm[...])
    loop(5, PER, relay)

    for p in range(2):
        @pl.when(xl == 1 - halves[p])
        def _():
            def other(t):
                s = 2 * t + 1 - core
                arrived(chunk(p, s), rsem.at[p, s])

            loop(0, PER, other)

    def swing_out(u):
        return remote(
            chunk(0, u, HALF), bo.at[aligned(u, CH), :], osend.at[u], osem.at[u], r, mate
        )

    for p in range(2):
        @pl.when(r == xl)
        def _():
            own = b[p, aligned(core, NB), :]
            if p == 0 and not same:
                own = choose(own, b[p, aligned(1 - core, NB), :], turned)
            b[p, bc_at, :] = own

        @pl.when((r == halves[p]) & (xl == 1 - halves[p]))
        def _():
            b[p, bc_at, :] = choose(ww[core, :NB, :], ww[core, NB:, :], odd[p]).T

        @pl.when((r == 1 - halves[p]) & (xl == halves[p]))
        def _():
            def below(u):
                arrived(chunk(p, u, HALF), bsem.at[p, u])
                if p == 0 and same:
                    swing_out(u).start()

            loop(0, PER, below)

    if not same:
        @pl.when(is_n)
        def _():
            loop(0, PER, lambda u: swing_out(u).start())

        @pl.when(r == h1)
        def _():
            pick_own()
    else:
        @pl.when((r == h1) & (xl == 1 - h1))
        def _():
            pick_own()

    def sink_pass(t):
        s = 2 * t + core
        return remote(
            chunk(0, s, HALF + NB), chunk(0, s, HALF + NB), gpass.at[t], gsem.at[s], r, mate
        )

    @pl.when(sink)
    def _():
        def take(t):
            s = 2 * t + core
            arrived(chunk(0, s, HALF + NB), gsem.at[s])
            sink_pass(t).start()

        def rest(t):
            s = 2 * t + 1 - core
            arrived(chunk(0, s, HALF + NB), gsem.at[s])

        loop(0, PER // 2, take)
        loop(0, PER // 2, rest)

    @pl.when(swing)
    def _():
        def gather(u):
            arrived(bo.at[aligned(u, CH), :], osem.at[u])

        loop(0, PER, gather)
        even_core = jnp.where(core == 0, 1.0, 0.0)
        b[0, g_at, :] = choose(
            b[0, bc_at, :], bo[...], even_core * odd[1] + (1 - even_core) * (1 - odd[1])
        )

    def product(rows, p):
        near = nt(rows[:, : NB // 2], inv[p, : NB // 2, : NB // 2])
        far = nt(rows, inv[p, NB // 2 :, :])
        return near.astype(BF16), far.astype(BF16)

    def keep(p, at, pieces):
        f[at, pl.ds(p * NB, NB // 2)] = pieces[0]
        f[at, pl.ds(p * NB + NB // 2, NB // 2)] = pieces[1]

    def first_factor(i):
        at = aligned(i, TILE)
        rows = b[0, at, :]
        if not same:
            flip = aligned(jnp.where(i < HALF // TILE, (i + 2) % 4, i), TILE)
            rows = choose(rows, b[0, flip, :], turned)
        keep(0, at, product(rows, 0))

    loop(0, 2 * HALF // TILE, first_factor)
    left = pl.ds(0, NB)
    right = pl.ds(NB, NB)

    def second_factor(i):
        at = aligned(i, TILE)
        part = b[1, at, :].astype(F32) - nt(f[at, left], f[g_at, left])
        keep(1, at, product(part.astype(BF16), 1))

    def solve(p):
        part = choose(field[:, :NB], field[:, NB:], odd[p])
        if p == 1:
            part = part - nt(solved[0], f[g_at, left])
        top, rest = split(part)
        solved[p] = (nt(top, inv[p]) + nt(rest, inv[p])).astype(BF16)

    def sharing(p):
        return remote(solved.at[p], solved.at[p], vsend.at[p], vsem.at[p], 1 - halves[p], c)

    def share(p):
        @pl.when(r == halves[p])
        def _():
            solve(p)
            sharing(p).start()

    def receive(p):
        @pl.when(r != halves[p])
        def _():
            arrived(solved.at[p], vsem.at[p])

    share(0)
    loop(0, 3 * NB // TILE, second_factor)
    receive(0)
    share(1)

    mine = pl.ds(pl.multiple_of(c * 128, 128), 128)
    mine_after = pl.ds(pl.multiple_of(c * 128 + NB, 128), 128)

    def finish(m):
        at = aligned(m, TILE)
        trail[0, at, :] = ww[core, at, :].astype(F32) - nt(f[at, :], f[bc_at, :])
        pans[0, 0, at, :] = f[at, mine]
        pans[0, 1, at, :] = f[at, mine_after]

    loop(0, HALF // TILE, finish)
    receive(1)

    def whiten(m):
        at = aligned(m, TILE)
        white[0, :, at] = field[:, at] - (
            nt(solved[0], f[at, left]) + nt(solved[1], f[at, right])
        )

    loop(0, HALF // TILE, whiten)

    @pl.when(swapper)
    def _():
        swapping().wait_send()

    for p in range(2):
        @pl.when(xl == halves[p])
        def _():
            loop(0, PER, lambda t: holding(p, t).wait_send())

        @pl.when(xl == 1 - halves[p])
        def _():
            loop(0, PER, lambda t: to_mate(p, t).wait_send())

            @pl.when(r == halves[p])
            def _():
                loop(0, PER, lambda t: to_down(p, t).wait_send())

        @pl.when(r == halves[p])
        def _():
            sharing(p).wait_send()

    @pl.when(source)
    def _():
        loop(0, PER // 2, lambda t: across(t).wait_send())

    @pl.when(sink)
    def _():
        loop(0, PER // 2, lambda t: sink_pass(t).wait_send())

    @pl.when(swing)
    def _():
        loop(0, PER, lambda u: swing_out(u).wait_send())

    loop(1, lat, lambda d: first(d).wait_send())
    loop(1, lat, lambda d: second(d).wait_send())


def solution(mesh):
    lat = mesh.shape["latent"]

    def local(observations, rotation, ordering, working, factor_inverse, panel_index):
        times, local_vars, stations = observations.shape
        steps = times // lat
        vmem = pl.BlockSpec(memory_space=pltpu.VMEM)
        anyw = pl.BlockSpec(memory_space=pl.ANY)
        dma = pltpu.SemaphoreType.DMA

        def call(halves, *operands):
            return pl.pallas_call(
                functools.partial(kernel, halves, lat),
                out_shape=(
                    jax.ShapeDtypeStruct((1, HALF, NB), F32),
                    jax.ShapeDtypeStruct((1, 2, HALF, 128), BF16),
                    jax.ShapeDtypeStruct((1, times, HALF), F32),
                ),
                in_specs=[pl.BlockSpec(memory_space=pltpu.SMEM)] + [anyw] * 5,
                out_specs=(vmem, vmem, vmem),
                scratch_shapes=[
                    pltpu.VMEM((2, NB, NB), BF16),
                    pltpu.VMEM((2, HALF, NB), BF16),
                    pltpu.VMEM((2, 2 * HALF, NB), BF16),
                    pltpu.VMEM((NB, NB), BF16),
                    pltpu.VMEM((2 * HALF, 2 * NB), BF16),
                    pltpu.VMEM((lat, steps, local_vars, HALF), BF16),
                    pltpu.VMEM((times * local_vars, HALF), F32),
                    pltpu.VMEM((lat, steps, HALF), F32),
                    pltpu.VMEM((lat, steps, HALF), F32),
                    pltpu.VMEM((times, HALF), F32),
                    pltpu.VMEM((HALF, HALF), BF16),
                    pltpu.VMEM((times, HALF), F32),
                    pltpu.VMEM((2, times, NB), BF16),
                    pltpu.VMEM(rotation.shape[::-1], F32),
                    pltpu.VMEM((1, HALF), jnp.int32),
                    dma((6,)),
                    dma((2,)),
                    dma((2, 2 * PER)),
                    dma((2, PER)),
                    dma((PER,)),
                    dma((PER,)),
                    dma((2,)),
                    dma((2, PER)),
                    dma((2, PER)),
                    dma((2, PER)),
                    dma((PER,)),
                    dma((PER // 2,)),
                    dma((PER // 2,)),
                    dma((2,)),
                    dma((lat,)),
                    dma((lat,)),
                    dma((lat,)),
                    dma((lat,)),
                ],
                compiler_params=pltpu.CompilerParams(
                    collective_id=halves[0] * 2 + halves[1], has_side_effects=True,
                    vmem_limit_bytes=48 << 20,
                ),
                name=f"panels_{halves[0]}{halves[1]}",
            )(*operands)

        branches = [functools.partial(call, (i, j)) for i in range(2) for j in range(2)]
        choice = jnp.sum((panel_index // 2) * jnp.array([2, 1], jnp.int32))
        return lax.switch(
            choice, branches,
            panel_index, observations, rotation.T, ordering.reshape(1, HALF), working,
            factor_inverse,
        )

    return jax.shard_map(
        local,
        mesh=mesh,
        in_specs=(
            P("col", "latent", "row"),
            P(),
            P("row"),
            P("latent", "row", "col"),
            P("latent", None, None, None),
            P(),
        ),
        out_specs=(
            P("latent", "row", "col"),
            P("latent", None, "row", "col"),
            P("latent", "col", "row"),
        ),
        check_vma=False,
    )
```

```python
import functools

import jax
import jax.numpy as jnp
from jax import lax
from jax.experimental import pallas as pl
from jax.experimental.pallas import tpu as pltpu
from jax.sharding import PartitionSpec as P

MESH = pl.DeviceIdType.MESH
F32 = jnp.float32
BF16 = jnp.bfloat16
NB = 512
HALF = 1024
PER = 8
CH = NB // PER
TILE = 256


def nt(a, b):
    return lax.dot_general(a, b, (((1,), (1,)), ((), ())), preferred_element_type=F32)


def nn(a, b):
    return jnp.dot(a, b, preferred_element_type=F32)


def split(value):
    high = value.astype(BF16)
    return high, (value - high.astype(F32)).astype(BF16)


def aligned(index, unit):
    return pl.ds(pl.multiple_of(index * unit, unit), unit)


def loop(start, stop, action):
    def step(i, carry):
        action(i)
        return carry

    lax.fori_loop(start, stop, step, 0)


def kernel(
    halves, equal, lat,
    which, obs, rot_hbm, order_hbm, w_hbm, inv_hbm,
    trail, pans, white,
    inv, ww, b, bo, f, fs, x, xf, y, z, zf, pm, field, solved, rot, order,
    lsem, swap, rsem, bsem, osem, gsem, vsem, hold, pair, down, osend, gsend, gpass, vsend,
    s1, r1, s2, r2,
):
    h0, h1 = halves
    same = h0 == h1
    moved = (0,) if equal else (0, 1)
    last = moved[-1]
    lid = lax.axis_index("latent")
    r = lax.axis_index("row")
    c = lax.axis_index("col")
    xl = c // 2
    core = c % 2
    mate = 2 * xl + 1 - core
    odd = [(which[p] & 1).astype(F32) for p in range(2)]
    steps = obs.shape[0] // lat
    local_vars = obs.shape[1]
    turned = jnp.where(r == h1, 1.0, 0.0) * odd[1]

    def choose(low, high, weight):
        mix = jnp.full(low.shape, weight, F32).astype(low.dtype)
        return low * (1 - mix) + high * mix

    def remote(src, dst, send, recv, row, col):
        return pltpu.make_async_remote_copy(
            src_ref=src, dst_ref=dst, send_sem=send, recv_sem=recv,
            device_id={"row": row, "col": col}, device_id_type=MESH,
        )

    def arrived(ref, sem):
        pltpu.make_async_copy(ref, ref, sem).wait()

    def chunk(p, s, base=0):
        return b.at[p, pl.ds(pl.multiple_of(base + s * CH, CH), CH), :]

    loads = [
        pltpu.make_async_copy(w_hbm.at[0], ww.at[core], lsem.at[0]),
        pltpu.make_async_copy(inv_hbm.at[0], inv, lsem.at[1]),
        pltpu.make_async_copy(obs.at[pl.ds(lid * steps, steps)], x.at[lid], lsem.at[2]),
        pltpu.make_async_copy(rot_hbm, rot, lsem.at[3]),
        pltpu.make_async_copy(order_hbm, order, lsem.at[4]),
    ]
    loads[0].start()
    for load in loads[1:]:
        load.start()

    barrier = pltpu.get_barrier_semaphore()

    def greet(d):
        pl.semaphore_signal(
            barrier, inc=1, device_id={"latent": lax.rem(lid + d, lat)}, device_id_type=MESH
        )

    def greet_group(d):
        other = lax.rem(r * 4 + c + d, 8)
        pl.semaphore_signal(
            barrier, inc=1, device_id={"row": other // 4, "col": other % 4}, device_id_type=MESH
        )

    loop(1, lat, greet)
    loop(1, 8, greet_group)
    pl.semaphore_wait(barrier, lat - 1 + 7)

    swapper = (xl == h0) | (xl == h1)

    def swapping(s):
        at = aligned(s, CH)
        return remote(
            w_hbm.at[0, at, :], ww.at[core, at, :], swap.at[0, s], swap.at[1, s], r, mate
        )

    def swapped(s):
        arrived(ww.at[1 - core, aligned(s, CH), :], swap.at[1, s])

    @pl.when(swapper)
    def _():
        def needed(u):
            swapping(2 * u + 1 - core).start()
            swapping(2 * u + 1 - core + PER).start()

        def others(u):
            swapping(2 * u + core).start()
            swapping(2 * u + core + PER).start()

        loop(0, PER // 2, needed)
        loop(0, PER // 2, others)

    def first(d):
        to = lax.rem(lid + d, lat)
        return pltpu.make_async_remote_copy(
            src_ref=obs.at[pl.ds(to * steps, steps)], dst_ref=x.at[lid],
            send_sem=s1.at[d], recv_sem=r1.at[d],
            device_id={"latent": to}, device_id_type=MESH,
        )

    def second(d):
        to = lax.rem(lid + d, lat)
        return pltpu.make_async_remote_copy(
            src_ref=y.at[to], dst_ref=z.at[lid],
            send_sem=s2.at[d], recv_sem=r2.at[d],
            device_id={"latent": to}, device_id_type=MESH,
        )

    loop(1, lat, lambda d: first(d).start())
    loads[0].wait()

    def holding(p, t):
        s = 2 * t + core
        return remote(chunk(p, s), chunk(p, s), hold.at[p, t], rsem.at[p, s], r, 2 * (1 - xl) + core)

    def stage(p, s):
        at = aligned(s, CH)
        value = choose(ww[0, at, :], ww[1, at, :], odd[p])
        if p == 0 and not same:
            flip = aligned((s + PER) % (2 * PER), CH)
            value = choose(value, choose(ww[0, flip, :], ww[1, flip, :], odd[p]), turned)
        b[p, at, :] = value

    def stage_all(s):
        for p in moved:
            @pl.when(xl == halves[p])
            def _():
                stage(p, s)

    def hold_all(t):
        for p in moved:
            @pl.when(xl == halves[p])
            def _():
                holding(p, t).start()

    @pl.when(swapper)
    def _():
        def early(u):
            swapped(2 * u + core)
            swapped(2 * u + core + PER)
            stage_all(2 * u + core)

            @pl.when(u > 0)
            def _():
                hold_all(u - 1)

        def late(t):
            stage_all(2 * t + core)
            hold_all(t - 1)

        loop(0, PER // 2, early)
        loop(PER // 2, PER, late)
        hold_all(PER - 1)

        def finish_swap(t):
            swapped(2 * t + 1 - core)

        loop(0, PER, finish_swap)
        loop(0, PER, lambda t: stage_all(2 * t + 1 - core))

    for load in loads[1:]:
        load.wait()

    is_n = (r == h0) & (xl == 1 - h0)
    source = (r == h1) & (xl == h1)
    sink = (r == 1 - h1) & (xl == 1 - h1)
    swing = (r == 1 - h1) & (xl == h1)
    g_at = pl.ds(HALF + NB, NB)
    bc_at = pl.ds(HALF, NB)

    def across(t):
        s = 2 * t + core
        src = chunk(0, s, HALF + NB) if same else chunk(0, s)
        return remote(
            src, chunk(0, s, HALF + NB), gsend.at[t], gsem.at[s], 1 - h1, 2 * (1 - h1) + core
        )

    def pick_own():
        if same:
            b[0, g_at, :] = choose(b[0, :NB, :], b[0, NB:HALF, :], odd[1])
        else:
            b[0, g_at, :] = b[0, :NB, :]

    if same:
        @pl.when(source)
        def _():
            pick_own()
            loop(0, PER // 2, lambda t: across(t).start())

    def swing_out(u):
        return remote(
            chunk(0, u, HALF), bo.at[aligned(u, CH), :], osend.at[u], osem.at[u], r, mate
        )

    for p in moved:
        @pl.when((r == halves[p]) & (xl == 1 - halves[p]))
        def _():
            b[p, bc_at, :] = choose(ww[core, :NB, :], ww[core, NB:, :], odd[p]).T

    if not same:
        @pl.when(is_n)
        def _():
            loop(0, PER, lambda u: swing_out(u).start())

    left = pl.ds(0, NB)
    right = pl.ds(NB, NB)
    place = order[...] - r * HALF

    def permutation(i):
        at = lax.broadcasted_iota(jnp.int32, (128, HALF), 0) + i * 128
        pm[aligned(i, 128), :] = jnp.where(at == place, 1.0, 0.0).astype(BF16)

    loop(0, HALF // 128, permutation)

    mixed_rows = lat * steps
    depth = lat * steps * local_vars
    total_vars = lat * local_vars
    pick_latent = (
        lax.broadcasted_iota(jnp.int32, (mixed_rows, lat), 0) // steps
        == lax.broadcasted_iota(jnp.int32, (mixed_rows, lat), 1)
    )
    pick_latent = jnp.where(pick_latent, 1.0, 0.0).astype(BF16)
    along = lax.broadcasted_iota(jnp.int32, (total_vars, depth), 1)
    pick_var = (along // (steps * local_vars)) * local_vars + along % local_vars
    pick_var = pick_var == lax.broadcasted_iota(jnp.int32, (total_vars, depth), 0)
    pick_var = jnp.where(pick_var, 1.0, 0.0).astype(BF16)
    wide = lax.broadcasted_iota(jnp.int32, (mixed_rows, depth), 1)
    tall = lax.broadcasted_iota(jnp.int32, (mixed_rows, depth), 0)
    same_step = (wide // local_vars) % steps == tall % steps

    def mixer(part):
        spread = nn(nn(pick_latent, part).astype(BF16), pick_var)
        return jnp.where(same_step, spread, 0.0).astype(BF16)

    rot_high, rot_low = split(rot[...])
    mix_high, mix_low = mixer(rot_high), mixer(rot_low)

    def to_mate(p, t):
        s = 2 * t + core
        return remote(chunk(p, s), chunk(p, s), pair.at[p, t], rsem.at[p, s], r, mate)

    def to_down(p, t):
        s = 2 * t + core
        return remote(
            chunk(p, s), chunk(p, s % PER, HALF), down.at[p, t], bsem.at[p, s % PER],
            1 - halves[p], 2 * halves[p] + s // PER,
        )

    def product(rows, p):
        near = nt(rows[:, : NB // 2], inv[p, : NB // 2, : NB // 2])
        far = nt(rows, inv[p, NB // 2 :, :])
        return near.astype(BF16), far.astype(BF16)

    def take_step(t):
        @pl.when(xl == 1 - h0)
        def _():
            s = 2 * t + 1 - core
            arrived(chunk(0, s), rsem.at[0, s])

        at = aligned(t, 2 * CH)
        near, far = product(b[0, at, :], 0)
        fs[at, : NB // 2] = near
        fs[at, NB // 2 :] = far

    def relay(t):
        pass_on(t)

        @pl.when(t > 0)
        def _():
            take_step(t - 1)

    def pass_on(t):
        s = 2 * t + core
        for p in moved:
            @pl.when(xl == 1 - halves[p])
            def _():
                arrived(chunk(p, s), rsem.at[p, s])
                to_mate(p, t).start()

                @pl.when(r == halves[p])
                def _():
                    to_down(p, t).start()

                if p == 0 and not same:
                    @pl.when((r == h1) & (t < PER // 2))
                    def _():
                        across(t).start()

    loop(0, 2, relay)
    loop(1, lat, lambda d: first(d).wait_recv())
    for i in range(lat):
        for t in range(steps):
            xf[pl.ds((i * steps + t) * local_vars, local_vars), :] = x[i, t].astype(F32)
    samples = xf[...].astype(BF16)
    mixed = nn(mix_high, samples) + nn(mix_low, samples)
    for i in range(lat):
        y[i] = mixed[i * steps : (i + 1) * steps]
    loop(1, lat, lambda d: second(d).start())
    own_z = pltpu.make_async_copy(y.at[lid], z.at[lid], lsem.at[5])
    own_z.start()
    loop(2, 5, relay)
    own_z.wait()
    loop(1, lat, lambda d: second(d).wait_recv())
    for i in range(lat):
        zf[pl.ds(i * steps, steps), :] = z[i]
    high, low = split(zf[...])
    field[...] = nn(high, pm[...]) + nn(low, pm[...])

    def solve(p):
        part = choose(field[:, :NB], field[:, NB:], odd[p])
        if p == 1:
            part = part - nt(solved[0], f[g_at, left])
        top, rest = split(part)
        solved[p] = (nt(top, inv[p]) + nt(rest, inv[p])).astype(BF16)

    def sharing(p):
        return remote(solved.at[p], solved.at[p], vsend.at[p], vsem.at[p], 1 - halves[p], c)

    def share(p):
        @pl.when(r == halves[p])
        def _():
            solve(p)
            sharing(p).start()

    def receive(p):
        @pl.when(r != halves[p])
        def _():
            arrived(solved.at[p], vsem.at[p])

    share(0)
    loop(5, PER, relay)
    take_step(PER - 1)

    if not equal:
        @pl.when(xl == 1 - h1)
        def _():
            def other(t):
                s = 2 * t + 1 - core
                arrived(chunk(1, s), rsem.at[1, s])

            loop(0, PER, other)

    for p in moved:
        @pl.when(r == xl)
        def _():
            own = b[p, aligned(core, NB), :]
            if p == 0 and not same:
                own = choose(own, b[p, aligned(1 - core, NB), :], turned)
            b[p, bc_at, :] = own

        @pl.when((r == 1 - halves[p]) & (xl == halves[p]))
        def _():
            def below(u):
                arrived(chunk(p, u, HALF), bsem.at[p, u])
                if p == 0 and same:
                    swing_out(u).start()

            loop(0, PER, below)

    if not same:
        @pl.when(r == h1)
        def _():
            pick_own()
    else:
        @pl.when((r == h1) & (xl == 1 - h1))
        def _():
            pick_own()

    def sink_pass(t):
        s = 2 * t + core
        return remote(
            chunk(0, s, HALF + NB), chunk(0, s, HALF + NB), gpass.at[t], gsem.at[s], r, mate
        )

    @pl.when(sink)
    def _():
        def take(t):
            s = 2 * t + core
            arrived(chunk(0, s, HALF + NB), gsem.at[s])
            sink_pass(t).start()

        def rest(t):
            s = 2 * t + 1 - core
            arrived(chunk(0, s, HALF + NB), gsem.at[s])

        loop(0, PER // 2, take)
        loop(0, PER // 2, rest)

    @pl.when(swing)
    def _():
        def gather(u):
            arrived(bo.at[aligned(u, CH), :], osem.at[u])

        loop(0, PER, gather)
        even_core = jnp.where(core == 0, 1.0, 0.0)
        b[0, g_at, :] = choose(
            b[0, bc_at, :], bo[...], even_core * odd[1] + (1 - even_core) * (1 - odd[1])
        )

    def keep(p, at, pieces):
        f[at, pl.ds(p * NB, NB // 2)] = pieces[0]
        f[at, pl.ds(p * NB + NB // 2, NB // 2)] = pieces[1]

    def first_factor(i):
        at = aligned(i, TILE)
        keep(0, at, product(b[0, at, :], 0))

    loop(HALF // TILE, 2 * HALF // TILE, first_factor)

    def settle(i):
        at = aligned(i, TILE)
        rows = fs[at, :]
        if not same:
            rows = choose(rows, fs[aligned((i + 2) % 4, TILE), :], turned)
        f[at, left] = rows

    loop(0, HALF // TILE, settle)

    def second_factor(i):
        at = aligned(i, TILE)
        part = b[last, at, :].astype(F32) - nt(f[at, left], f[g_at, left])
        keep(1, at, product(part.astype(BF16), 1))

    receive(0)
    share(1)
    loop(0, 3 * NB // TILE, second_factor)

    mine = pl.ds(pl.multiple_of(c * 128, 128), 128)
    mine_after = pl.ds(pl.multiple_of(c * 128 + NB, 128), 128)

    def finish(m):
        at = aligned(m, TILE)
        trail[0, at, :] = ww[core, at, :].astype(F32) - nt(f[at, :], f[bc_at, :])
        pans[0, 0, at, :] = f[at, mine]
        pans[0, 1, at, :] = f[at, mine_after]

    loop(0, HALF // TILE, finish)
    receive(1)

    def whiten(m):
        at = aligned(m, TILE)
        white[0, :, at] = field[:, at] - (
            nt(solved[0], f[at, left]) + nt(solved[1], f[at, right])
        )

    loop(0, HALF // TILE, whiten)

    @pl.when(swapper)
    def _():
        loop(0, 2 * PER, lambda s: swapping(s).wait_send())

    for p in moved:
        @pl.when(xl == halves[p])
        def _():
            loop(0, PER, lambda t: holding(p, t).wait_send())

        @pl.when(xl == 1 - halves[p])
        def _():
            loop(0, PER, lambda t: to_mate(p, t).wait_send())

            @pl.when(r == halves[p])
            def _():
                loop(0, PER, lambda t: to_down(p, t).wait_send())

    for p in range(2):
        @pl.when(r == halves[p])
        def _():
            sharing(p).wait_send()

    @pl.when(source)
    def _():
        loop(0, PER // 2, lambda t: across(t).wait_send())

    @pl.when(sink)
    def _():
        loop(0, PER // 2, lambda t: sink_pass(t).wait_send())

    @pl.when(swing)
    def _():
        loop(0, PER, lambda u: swing_out(u).wait_send())

    loop(1, lat, lambda d: first(d).wait_send())
    loop(1, lat, lambda d: second(d).wait_send())


def solution(mesh):
    lat = mesh.shape["latent"]

    def local(observations, rotation, ordering, working, factor_inverse, panel_index):
        times, local_vars, stations = observations.shape
        steps = times // lat
        vmem = pl.BlockSpec(memory_space=pltpu.VMEM)
        anyw = pl.BlockSpec(memory_space=pl.ANY)
        dma = pltpu.SemaphoreType.DMA

        def call(halves, equal, *operands):
            return pl.pallas_call(
                functools.partial(kernel, halves, equal, lat),
                out_shape=(
                    jax.ShapeDtypeStruct((1, HALF, NB), F32),
                    jax.ShapeDtypeStruct((1, 2, HALF, 128), BF16),
                    jax.ShapeDtypeStruct((1, times, HALF), F32),
                ),
                in_specs=[pl.BlockSpec(memory_space=pltpu.SMEM)] + [anyw] * 5,
                out_specs=(vmem, vmem, vmem),
                scratch_shapes=[
                    pltpu.VMEM((2, NB, NB), BF16),
                    pltpu.VMEM((2, HALF, NB), BF16),
                    pltpu.VMEM((2, 2 * HALF, NB), BF16),
                    pltpu.VMEM((NB, NB), BF16),
                    pltpu.VMEM((2 * HALF, 2 * NB), BF16),
                    pltpu.VMEM((HALF, NB), BF16),
                    pltpu.VMEM((lat, steps, local_vars, HALF), BF16),
                    pltpu.VMEM((times * local_vars, HALF), F32),
                    pltpu.VMEM((lat, steps, HALF), F32),
                    pltpu.VMEM((lat, steps, HALF), F32),
                    pltpu.VMEM((times, HALF), F32),
                    pltpu.VMEM((HALF, HALF), BF16),
                    pltpu.VMEM((times, HALF), F32),
                    pltpu.VMEM((2, times, NB), BF16),
                    pltpu.VMEM(rotation.shape[::-1], F32),
                    pltpu.VMEM((1, HALF), jnp.int32),
                    dma((6,)),
                    dma((2, 2 * PER)),
                    dma((2, 2 * PER)),
                    dma((2, PER)),
                    dma((PER,)),
                    dma((PER,)),
                    dma((2,)),
                    dma((2, PER)),
                    dma((2, PER)),
                    dma((2, PER)),
                    dma((PER,)),
                    dma((PER // 2,)),
                    dma((PER // 2,)),
                    dma((2,)),
                    dma((lat,)),
                    dma((lat,)),
                    dma((lat,)),
                    dma((lat,)),
                ],
                compiler_params=pltpu.CompilerParams(
                    collective_id=4 + halves[0] if equal else halves[0] * 2 + halves[1], has_side_effects=True,
                    vmem_limit_bytes=48 << 20,
                ),
                name=f"panels_{halves[0]}{halves[1]}{int(equal)}",
            )(*operands)

        branches = [functools.partial(call, (i, j), False) for i in range(2) for j in range(2)]
        branches += [functools.partial(call, (i, i), True) for i in range(2)]
        code = jnp.sum(panel_index * jnp.array([4, 1], jnp.int32))
        upper, lower = code >> 3, (code >> 1) & 1
        choice = jnp.where(lax.rem(code, 5) == 0, 4 + upper, upper * 2 + lower)
        return lax.switch(
            choice, branches,
            panel_index, observations, rotation.T, ordering.reshape(1, HALF), working,
            factor_inverse,
        )

    return jax.shard_map(
        local,
        mesh=mesh,
        in_specs=(
            P("col", "latent", "row"),
            P(),
            P("row"),
            P("latent", "row", "col"),
            P("latent", None, None, None),
            P(),
        ),
        out_specs=(
            P("latent", "row", "col"),
            P("latent", None, "row", "col"),
            P("latent", "col", "row"),
        ),
        check_vma=False,
    )
```

```python
import functools

import jax
import jax.numpy as jnp
from jax import lax
from jax.experimental import pallas as pl
from jax.experimental.pallas import tpu as pltpu
from jax.sharding import PartitionSpec as P

MESH = pl.DeviceIdType.MESH
F32 = jnp.float32
BF16 = jnp.bfloat16
NB = 512
HALF = 1024
PER = 8
CH = NB // PER
TILE = 512


def nt(a, b):
    return lax.dot_general(a, b, (((1,), (1,)), ((), ())), preferred_element_type=F32)


def nn(a, b):
    return jnp.dot(a, b, preferred_element_type=F32)


def split(value):
    high = value.astype(BF16)
    return high, (value - high.astype(F32)).astype(BF16)


def aligned(index, unit):
    return pl.ds(pl.multiple_of(index * unit, unit), unit)


def loop(start, stop, action):
    def step(i, carry):
        action(i)
        return carry

    lax.fori_loop(start, stop, step, 0)


def kernel(
    halves, equal, lat,
    which, obs, rot_hbm, order_hbm, w_hbm, inv_hbm,
    trail, pans, white,
    inv, ww, b, bo, f, fs, x, xf, y, z, zf, pm, field, solved, rot, order,
    lsem, swap, rsem, bsem, osem, gsem, vsem, hold, pair, down, osend, gsend, gpass, vsend,
    s1, r1, s2, r2,
):
    h0, h1 = halves
    same = h0 == h1
    moved = (0,) if equal else (0, 1)
    last = moved[-1]
    lid = lax.axis_index("latent")
    r = lax.axis_index("row")
    c = lax.axis_index("col")
    xl = c // 2
    core = c % 2
    mate = 2 * xl + 1 - core
    odd = [(which[p] & 1).astype(F32) for p in range(2)]
    steps = obs.shape[0] // lat
    local_vars = obs.shape[1]
    turned = jnp.where(r == h1, 1.0, 0.0) * odd[1]

    def choose(low, high, weight):
        mix = jnp.full(low.shape, weight, F32).astype(low.dtype)
        return low * (1 - mix) + high * mix

    def remote(src, dst, send, recv, row, col):
        return pltpu.make_async_remote_copy(
            src_ref=src, dst_ref=dst, send_sem=send, recv_sem=recv,
            device_id={"row": row, "col": col}, device_id_type=MESH,
        )

    def arrived(ref, sem):
        pltpu.make_async_copy(ref, ref, sem).wait()

    def chunk(p, s, base=0):
        return b.at[p, pl.ds(pl.multiple_of(base + s * CH, CH), CH), :]

    loads = [
        pltpu.make_async_copy(w_hbm.at[0], ww.at[core], lsem.at[0]),
        pltpu.make_async_copy(inv_hbm.at[0], inv, lsem.at[1]),
        pltpu.make_async_copy(obs.at[pl.ds(lid * steps, steps)], x.at[lid], lsem.at[2]),
        pltpu.make_async_copy(rot_hbm, rot, lsem.at[3]),
        pltpu.make_async_copy(order_hbm, order, lsem.at[4]),
    ]
    loads[0].start()
    for load in loads[1:]:
        load.start()

    barrier = pltpu.get_barrier_semaphore()

    def greet(d):
        pl.semaphore_signal(
            barrier, inc=1, device_id={"latent": lax.rem(lid + d, lat)}, device_id_type=MESH
        )

    def greet_group(d):
        other = lax.rem(r * 4 + c + d, 8)
        pl.semaphore_signal(
            barrier, inc=1, device_id={"row": other // 4, "col": other % 4}, device_id_type=MESH
        )

    loop(1, lat, greet)
    loop(1, 8, greet_group)
    pl.semaphore_wait(barrier, lat - 1 + 7)

    swapper = (xl == h0) | (xl == h1)

    def swapping(s):
        at = aligned(s, CH)
        return remote(
            w_hbm.at[0, at, :], ww.at[core, at, :], swap.at[0, s], swap.at[1, s], r, mate
        )

    def swapped(s):
        arrived(ww.at[1 - core, aligned(s, CH), :], swap.at[1, s])

    @pl.when(swapper)
    def _():
        def needed(u):
            swapping(2 * u + 1 - core).start()
            swapping(2 * u + 1 - core + PER).start()

        def others(u):
            swapping(2 * u + core).start()
            swapping(2 * u + core + PER).start()

        loop(0, PER // 2, needed)
        loop(0, PER // 2, others)

    def first(d):
        to = lax.rem(lid + d, lat)
        return pltpu.make_async_remote_copy(
            src_ref=obs.at[pl.ds(to * steps, steps)], dst_ref=x.at[lid],
            send_sem=s1.at[d], recv_sem=r1.at[d],
            device_id={"latent": to}, device_id_type=MESH,
        )

    def second(d):
        to = lax.rem(lid + d, lat)
        return pltpu.make_async_remote_copy(
            src_ref=y.at[to], dst_ref=z.at[lid],
            send_sem=s2.at[d], recv_sem=r2.at[d],
            device_id={"latent": to}, device_id_type=MESH,
        )

    loop(1, lat, lambda d: first(d).start())
    loads[0].wait()

    def holding(p, t):
        s = 2 * t + core
        return remote(chunk(p, s), chunk(p, s), hold.at[p, t], rsem.at[p, s], r, 2 * (1 - xl) + core)

    def stage(p, s):
        at = aligned(s, CH)
        value = choose(ww[0, at, :], ww[1, at, :], odd[p])
        if p == 0 and not same:
            flip = aligned((s + PER) % (2 * PER), CH)
            value = choose(value, choose(ww[0, flip, :], ww[1, flip, :], odd[p]), turned)
        b[p, at, :] = value

    def stage_all(s):
        for p in moved:
            @pl.when(xl == halves[p])
            def _():
                stage(p, s)

    def hold_all(t):
        for p in moved:
            @pl.when(xl == halves[p])
            def _():
                holding(p, t).start()

    @pl.when(swapper)
    def _():
        def early(u):
            swapped(2 * u + core)
            swapped(2 * u + core + PER)
            stage_all(2 * u + core)

            @pl.when(u > 0)
            def _():
                hold_all(u - 1)

        def late(t):
            stage_all(2 * t + core)
            hold_all(t - 1)

        loop(0, PER // 2, early)
        loop(PER // 2, PER, late)
        hold_all(PER - 1)

        def finish_swap(t):
            swapped(2 * t + 1 - core)

        loop(0, PER, finish_swap)
        loop(0, PER, lambda t: stage_all(2 * t + 1 - core))

    for load in loads[1:]:
        load.wait()

    is_n = (r == h0) & (xl == 1 - h0)
    source = (r == h1) & (xl == h1)
    sink = (r == 1 - h1) & (xl == 1 - h1)
    swing = (r == 1 - h1) & (xl == h1)
    g_at = pl.ds(HALF + NB, NB)
    bc_at = pl.ds(HALF, NB)

    def across(t):
        s = 2 * t + core
        src = chunk(0, s, HALF + NB) if same else chunk(0, s)
        return remote(
            src, chunk(0, s, HALF + NB), gsend.at[t], gsem.at[s], 1 - h1, 2 * (1 - h1) + core
        )

    def pick_own():
        if same:
            b[0, g_at, :] = choose(b[0, :NB, :], b[0, NB:HALF, :], odd[1])
        else:
            b[0, g_at, :] = b[0, :NB, :]

    if same:
        @pl.when(source)
        def _():
            pick_own()
            loop(0, PER // 2, lambda t: across(t).start())

    def swing_out(u):
        return remote(
            chunk(0, u, HALF), bo.at[aligned(u, CH), :], osend.at[u], osem.at[u], r, mate
        )

    for p in moved:
        @pl.when((r == halves[p]) & (xl == 1 - halves[p]))
        def _():
            b[p, bc_at, :] = choose(ww[core, :NB, :], ww[core, NB:, :], odd[p]).T

    if not same:
        @pl.when(is_n)
        def _():
            loop(0, PER, lambda u: swing_out(u).start())

    left = pl.ds(0, NB)
    right = pl.ds(NB, NB)
    place = order[...] - r * HALF

    def permutation(i):
        at = lax.broadcasted_iota(jnp.int32, (128, HALF), 0) + i * 128
        pm[aligned(i, 128), :] = jnp.where(at == place, 1.0, 0.0).astype(BF16)

    loop(0, HALF // 128, permutation)

    mixed_rows = lat * steps
    depth = lat * steps * local_vars
    total_vars = lat * local_vars
    pick_latent = (
        lax.broadcasted_iota(jnp.int32, (mixed_rows, lat), 0) // steps
        == lax.broadcasted_iota(jnp.int32, (mixed_rows, lat), 1)
    )
    pick_latent = jnp.where(pick_latent, 1.0, 0.0).astype(BF16)
    along = lax.broadcasted_iota(jnp.int32, (total_vars, depth), 1)
    pick_var = (along // (steps * local_vars)) * local_vars + along % local_vars
    pick_var = pick_var == lax.broadcasted_iota(jnp.int32, (total_vars, depth), 0)
    pick_var = jnp.where(pick_var, 1.0, 0.0).astype(BF16)
    wide = lax.broadcasted_iota(jnp.int32, (mixed_rows, depth), 1)
    tall = lax.broadcasted_iota(jnp.int32, (mixed_rows, depth), 0)
    same_step = (wide // local_vars) % steps == tall % steps

    def mixer(part):
        spread = nn(nn(pick_latent, part).astype(BF16), pick_var)
        return jnp.where(same_step, spread, 0.0).astype(BF16)

    rot_high, rot_low = split(rot[...])
    mix_high, mix_low = mixer(rot_high), mixer(rot_low)

    def to_mate(p, t):
        s = 2 * t + core
        return remote(chunk(p, s), chunk(p, s), pair.at[p, t], rsem.at[p, s], r, mate)

    def to_down(p, t):
        s = 2 * t + core
        return remote(
            chunk(p, s), chunk(p, s % PER, HALF), down.at[p, t], bsem.at[p, s % PER],
            1 - halves[p], 2 * halves[p] + s // PER,
        )

    def product(rows, p):
        near = nt(rows[:, : NB // 2], inv[p, : NB // 2, : NB // 2])
        far = nt(rows, inv[p, NB // 2 :, :])
        return near.astype(BF16), far.astype(BF16)

    def take_step(t):
        @pl.when(xl == 1 - h0)
        def _():
            s = 2 * t + 1 - core
            arrived(chunk(0, s), rsem.at[0, s])

        @pl.when(t % 2 == 1)
        def _():
            at = aligned(t // 2, 4 * CH)
            near, far = product(b[0, at, :], 0)
            fs[at, : NB // 2] = near
            fs[at, NB // 2 :] = far

    def relay(t):
        pass_on(t)

        @pl.when(t > 0)
        def _():
            take_step(t - 1)

    def pass_on(t):
        s = 2 * t + core
        for p in moved:
            @pl.when(xl == 1 - halves[p])
            def _():
                arrived(chunk(p, s), rsem.at[p, s])
                to_mate(p, t).start()

                @pl.when(r == halves[p])
                def _():
                    to_down(p, t).start()

                if p == 0 and not same:
                    @pl.when((r == h1) & (t < PER // 2))
                    def _():
                        across(t).start()

    loop(0, 2, relay)
    loop(1, lat, lambda d: first(d).wait_recv())
    for i in range(lat):
        for t in range(steps):
            xf[pl.ds((i * steps + t) * local_vars, local_vars), :] = x[i, t].astype(F32)
    samples = xf[...].astype(BF16)
    mixed = nn(mix_high, samples) + nn(mix_low, samples)
    for i in range(lat):
        y[i] = mixed[i * steps : (i + 1) * steps]
    loop(1, lat, lambda d: second(d).start())
    own_z = pltpu.make_async_copy(y.at[lid], z.at[lid], lsem.at[5])
    own_z.start()
    loop(2, 5, relay)
    own_z.wait()
    loop(1, lat, lambda d: second(d).wait_recv())
    for i in range(lat):
        zf[pl.ds(i * steps, steps), :] = z[i]
    high, low = split(zf[...])
    field[...] = nn(high, pm[...]) + nn(low, pm[...])

    def solve(p):
        part = choose(field[:, :NB], field[:, NB:], odd[p])
        if p == 1:
            part = part - nt(solved[0], f[g_at, left])
        top, rest = split(part)
        solved[p] = (nt(top, inv[p]) + nt(rest, inv[p])).astype(BF16)

    def sharing(p):
        return remote(solved.at[p], solved.at[p], vsend.at[p], vsem.at[p], 1 - halves[p], c)

    def share(p):
        @pl.when(r == halves[p])
        def _():
            solve(p)
            sharing(p).start()

    def receive(p):
        @pl.when(r != halves[p])
        def _():
            arrived(solved.at[p], vsem.at[p])

    share(0)
    loop(5, PER, relay)
    take_step(PER - 1)

    if not equal:
        @pl.when(xl == 1 - h1)
        def _():
            def other(t):
                s = 2 * t + 1 - core
                arrived(chunk(1, s), rsem.at[1, s])

            loop(0, PER, other)

    for p in moved:
        @pl.when(r == xl)
        def _():
            own = b[p, aligned(core, NB), :]
            if p == 0 and not same:
                own = choose(own, b[p, aligned(1 - core, NB), :], turned)
            b[p, bc_at, :] = own

        @pl.when((r == 1 - halves[p]) & (xl == halves[p]))
        def _():
            def below(u):
                arrived(chunk(p, u, HALF), bsem.at[p, u])
                if p == 0 and same:
                    swing_out(u).start()

            loop(0, PER, below)

    if not same:
        @pl.when(r == h1)
        def _():
            pick_own()
    else:
        @pl.when((r == h1) & (xl == 1 - h1))
        def _():
            pick_own()

    def sink_pass(t):
        s = 2 * t + core
        return remote(
            chunk(0, s, HALF + NB), chunk(0, s, HALF + NB), gpass.at[t], gsem.at[s], r, mate
        )

    @pl.when(sink)
    def _():
        def take(t):
            s = 2 * t + core
            arrived(chunk(0, s, HALF + NB), gsem.at[s])
            sink_pass(t).start()

        def rest(t):
            s = 2 * t + 1 - core
            arrived(chunk(0, s, HALF + NB), gsem.at[s])

        loop(0, PER // 2, take)
        loop(0, PER // 2, rest)

    @pl.when(swing)
    def _():
        def gather(u):
            arrived(bo.at[aligned(u, CH), :], osem.at[u])

        loop(0, PER, gather)
        even_core = jnp.where(core == 0, 1.0, 0.0)
        b[0, g_at, :] = choose(
            b[0, bc_at, :], bo[...], even_core * odd[1] + (1 - even_core) * (1 - odd[1])
        )

    def keep(p, at, pieces):
        f[at, pl.ds(p * NB, NB // 2)] = pieces[0]
        f[at, pl.ds(p * NB + NB // 2, NB // 2)] = pieces[1]

    def first_factor(i):
        at = aligned(i, TILE)
        keep(0, at, product(b[0, at, :], 0))

    loop(HALF // TILE, 2 * HALF // TILE, first_factor)

    def settle(i):
        at = aligned(i, TILE)
        rows = fs[at, :]
        if not same:
            rows = choose(rows, fs[aligned((i + NB // TILE) % (HALF // TILE), TILE), :], turned)
        f[at, left] = rows

    loop(0, HALF // TILE, settle)

    def second_factor(i):
        at = aligned(i, TILE)
        part = b[last, at, :].astype(F32) - nt(f[at, left], f[g_at, left])
        keep(1, at, product(part.astype(BF16), 1))

    receive(0)
    share(1)
    loop(0, 3 * NB // TILE, second_factor)

    mine = pl.ds(pl.multiple_of(c * 128, 128), 128)
    mine_after = pl.ds(pl.multiple_of(c * 128 + NB, 128), 128)

    def finish(m):
        at = aligned(m, TILE)
        trail[0, at, :] = ww[core, at, :].astype(F32) - nt(f[at, :], f[bc_at, :])
        pans[0, 0, at, :] = f[at, mine]
        pans[0, 1, at, :] = f[at, mine_after]

    loop(0, HALF // TILE, finish)
    receive(1)

    def whiten(m):
        at = aligned(m, TILE)
        white[0, :, at] = field[:, at] - (
            nt(solved[0], f[at, left]) + nt(solved[1], f[at, right])
        )

    loop(0, HALF // TILE, whiten)

    @pl.when(swapper)
    def _():
        loop(0, 2 * PER, lambda s: swapping(s).wait_send())

    for p in moved:
        @pl.when(xl == halves[p])
        def _():
            loop(0, PER, lambda t: holding(p, t).wait_send())

        @pl.when(xl == 1 - halves[p])
        def _():
            loop(0, PER, lambda t: to_mate(p, t).wait_send())

            @pl.when(r == halves[p])
            def _():
                loop(0, PER, lambda t: to_down(p, t).wait_send())

    for p in range(2):
        @pl.when(r == halves[p])
        def _():
            sharing(p).wait_send()

    @pl.when(source)
    def _():
        loop(0, PER // 2, lambda t: across(t).wait_send())

    @pl.when(sink)
    def _():
        loop(0, PER // 2, lambda t: sink_pass(t).wait_send())

    @pl.when(swing)
    def _():
        loop(0, PER, lambda u: swing_out(u).wait_send())

    loop(1, lat, lambda d: first(d).wait_send())
    loop(1, lat, lambda d: second(d).wait_send())


def solution(mesh):
    lat = mesh.shape["latent"]

    def local(observations, rotation, ordering, working, factor_inverse, panel_index):
        times, local_vars, stations = observations.shape
        steps = times // lat
        vmem = pl.BlockSpec(memory_space=pltpu.VMEM)
        anyw = pl.BlockSpec(memory_space=pl.ANY)
        dma = pltpu.SemaphoreType.DMA

        def call(halves, equal, *operands):
            return pl.pallas_call(
                functools.partial(kernel, halves, equal, lat),
                out_shape=(
                    jax.ShapeDtypeStruct((1, HALF, NB), F32),
                    jax.ShapeDtypeStruct((1, 2, HALF, 128), BF16),
                    jax.ShapeDtypeStruct((1, times, HALF), F32),
                ),
                in_specs=[pl.BlockSpec(memory_space=pltpu.SMEM)] + [anyw] * 5,
                out_specs=(vmem, vmem, vmem),
                scratch_shapes=[
                    pltpu.VMEM((2, NB, NB), BF16),
                    pltpu.VMEM((2, HALF, NB), BF16),
                    pltpu.VMEM((2, 2 * HALF, NB), BF16),
                    pltpu.VMEM((NB, NB), BF16),
                    pltpu.VMEM((2 * HALF, 2 * NB), BF16),
                    pltpu.VMEM((HALF, NB), BF16),
                    pltpu.VMEM((lat, steps, local_vars, HALF), BF16),
                    pltpu.VMEM((times * local_vars, HALF), F32),
                    pltpu.VMEM((lat, steps, HALF), F32),
                    pltpu.VMEM((lat, steps, HALF), F32),
                    pltpu.VMEM((times, HALF), F32),
                    pltpu.VMEM((HALF, HALF), BF16),
                    pltpu.VMEM((times, HALF), F32),
                    pltpu.VMEM((2, times, NB), BF16),
                    pltpu.VMEM(rotation.shape[::-1], F32),
                    pltpu.VMEM((1, HALF), jnp.int32),
                    dma((6,)),
                    dma((2, 2 * PER)),
                    dma((2, 2 * PER)),
                    dma((2, PER)),
                    dma((PER,)),
                    dma((PER,)),
                    dma((2,)),
                    dma((2, PER)),
                    dma((2, PER)),
                    dma((2, PER)),
                    dma((PER,)),
                    dma((PER // 2,)),
                    dma((PER // 2,)),
                    dma((2,)),
                    dma((lat,)),
                    dma((lat,)),
                    dma((lat,)),
                    dma((lat,)),
                ],
                compiler_params=pltpu.CompilerParams(
                    collective_id=4 + halves[0] if equal else halves[0] * 2 + halves[1], has_side_effects=True,
                    vmem_limit_bytes=48 << 20,
                ),
                name=f"panels_{halves[0]}{halves[1]}{int(equal)}",
            )(*operands)

        branches = [functools.partial(call, (i, j), False) for i in range(2) for j in range(2)]
        branches += [functools.partial(call, (i, i), True) for i in range(2)]
        code = jnp.sum(panel_index * jnp.array([4, 1], jnp.int32))
        upper, lower = code >> 3, (code >> 1) & 1
        choice = jnp.where(lax.rem(code, 5) == 0, 4 + upper, upper * 2 + lower)
        return lax.switch(
            choice, branches,
            panel_index, observations, rotation.T, ordering.reshape(1, HALF), working,
            factor_inverse,
        )

    return jax.shard_map(
        local,
        mesh=mesh,
        in_specs=(
            P("col", "latent", "row"),
            P(),
            P("row"),
            P("latent", "row", "col"),
            P("latent", None, None, None),
            P(),
        ),
        out_specs=(
            P("latent", "row", "col"),
            P("latent", None, "row", "col"),
            P("latent", "col", "row"),
        ),
        check_vma=False,
    )
```

```python
import functools

import jax
import jax.numpy as jnp
from jax import lax
from jax.experimental import pallas as pl
from jax.experimental.pallas import tpu as pltpu
from jax.sharding import PartitionSpec as P

MESH = pl.DeviceIdType.MESH
F32 = jnp.float32
BF16 = jnp.bfloat16
NB = 512
HALF = 1024
PER = 8
CH = NB // PER
TILE = 512
FAR = PER - 2


def nt(a, b):
    return lax.dot_general(a, b, (((1,), (1,)), ((), ())), preferred_element_type=F32)


def nn(a, b):
    return jnp.dot(a, b, preferred_element_type=F32)


def split(value):
    high = value.astype(BF16)
    return high, (value - high.astype(F32)).astype(BF16)


def aligned(index, unit):
    return pl.ds(pl.multiple_of(index * unit, unit), unit)


def loop(start, stop, action):
    def step(i, carry):
        action(i)
        return carry

    lax.fori_loop(start, stop, step, 0)


def kernel(
    halves, equal, lat,
    which, obs, rot_hbm, order_hbm, w_hbm, inv_hbm,
    trail, pans, white,
    inv, ww, b, bo, tb, f, fs, x, xf, y, z, zf, pm, field, solved, rot, order,
    lsem, swap, rsem, bsem, osem, gsem, vsem, hold, pair, down, osend, gsend, gpass, vsend, far, fsend, dsend,
    s1, r1, s2, r2,
):
    h0, h1 = halves
    same = h0 == h1
    moved = (0,) if equal else (0, 1)
    last = moved[-1]
    lid = lax.axis_index("latent")
    r = lax.axis_index("row")
    c = lax.axis_index("col")
    xl = c // 2
    core = c % 2
    mate = 2 * xl + 1 - core
    odd = [(which[p] & 1).astype(F32) for p in range(2)]
    steps = obs.shape[0] // lat
    local_vars = obs.shape[1]
    turned = jnp.where(r == h1, 1.0, 0.0) * odd[1]

    def choose(low, high, weight):
        mix = jnp.full(low.shape, weight, F32).astype(low.dtype)
        return low * (1 - mix) + high * mix

    def remote(src, dst, send, recv, row, col):
        return pltpu.make_async_remote_copy(
            src_ref=src, dst_ref=dst, send_sem=send, recv_sem=recv,
            device_id={"row": row, "col": col}, device_id_type=MESH,
        )

    def arrived(ref, sem):
        pltpu.make_async_copy(ref, ref, sem).wait()

    def chunk(p, s, base=0):
        return b.at[p, pl.ds(pl.multiple_of(base + s * CH, CH), CH), :]

    loads = [
        pltpu.make_async_copy(w_hbm.at[0], ww.at[core], lsem.at[0]),
        pltpu.make_async_copy(inv_hbm.at[0], inv, lsem.at[1]),
        pltpu.make_async_copy(obs.at[pl.ds(lid * steps, steps)], x.at[lid], lsem.at[2]),
        pltpu.make_async_copy(rot_hbm, rot, lsem.at[3]),
        pltpu.make_async_copy(order_hbm, order, lsem.at[4]),
    ]
    loads[0].start()
    for load in loads[1:]:
        load.start()

    barrier = pltpu.get_barrier_semaphore()

    def greet(d):
        pl.semaphore_signal(
            barrier, inc=1, device_id={"latent": lax.rem(lid + d, lat)}, device_id_type=MESH
        )

    def greet_group(d):
        other = lax.rem(r * 4 + c + d, 8)
        pl.semaphore_signal(
            barrier, inc=1, device_id={"row": other // 4, "col": other % 4}, device_id_type=MESH
        )

    loop(1, lat, greet)
    loop(1, 8, greet_group)
    pl.semaphore_wait(barrier, lat - 1 + 7)

    swapper = (xl == h0) | (xl == h1)

    def swapping(s):
        at = aligned(s, CH)
        return remote(
            w_hbm.at[0, at, :], ww.at[core, at, :], swap.at[0, s], swap.at[1, s], r, mate
        )

    def swapped(s):
        arrived(ww.at[1 - core, aligned(s, CH), :], swap.at[1, s])

    @pl.when(swapper)
    def _():
        def needed(u):
            swapping(2 * u + 1 - core).start()
            swapping(2 * u + 1 - core + PER).start()

        def others(u):
            swapping(2 * u + core).start()
            swapping(2 * u + core + PER).start()

        loop(0, PER // 2, needed)
        loop(0, PER // 2, others)

    def first(d):
        to = lax.rem(lid + d, lat)
        return pltpu.make_async_remote_copy(
            src_ref=obs.at[pl.ds(to * steps, steps)], dst_ref=x.at[lid],
            send_sem=s1.at[d], recv_sem=r1.at[d],
            device_id={"latent": to}, device_id_type=MESH,
        )

    def second(d):
        to = lax.rem(lid + d, lat)
        return pltpu.make_async_remote_copy(
            src_ref=y.at[to], dst_ref=z.at[lid],
            send_sem=s2.at[d], recv_sem=r2.at[d],
            device_id={"latent": to}, device_id_type=MESH,
        )

    loop(1, lat, lambda d: first(d).start())
    loads[0].wait()

    def holding(p, t):
        s = 2 * t + core
        return remote(chunk(p, s), chunk(p, s), hold.at[p, t], rsem.at[p, s], r, 2 * (1 - xl) + core)

    def stage(p, s):
        at = aligned(s, CH)
        value = choose(ww[0, at, :], ww[1, at, :], odd[p])
        if p == 0 and not same:
            flip = aligned((s + PER) % (2 * PER), CH)
            value = choose(value, choose(ww[0, flip, :], ww[1, flip, :], odd[p]), turned)
        b[p, at, :] = value

    def stage_all(s):
        for p in moved:
            @pl.when(xl == halves[p])
            def _():
                stage(p, s)

    def holding_far(p, k):
        return remote(
            chunk(p, 2 * (FAR + k) + core), tb.at[p, k], hold.at[p, FAR + k], far.at[p, k],
            1 - r, 2 * (1 - xl) + core,
        )

    def hold_all(t):
        for p in moved:
            near = (xl == halves[p]) & (t < FAR) if same else xl == halves[p]

            @pl.when(near)
            def _():
                holding(p, t).start()

            if same:
                @pl.when((xl == h0) & (t >= FAR))
                def _():
                    holding_far(p, t - FAR).start()

    def transit(p, k):
        s = 2 * (FAR + k) + core
        src, sem = tb.at[p, k], fsend.at[p, k]
        to_d = remote(
            src, chunk(p, s - PER, HALF), sem, bsem.at[p, s - PER], 1 - h0, 2 * h0 + 1
        )
        to_s = remote(src, tb.at[p, k], sem, far.at[p, k], h0, 2 * h0 + core)
        to_t = remote(src, chunk(p, s), sem, rsem.at[p, s], 1 - h0, 2 * (1 - h0) + core)
        return to_d, to_s, to_t

    def upward(p, u):
        return remote(
            chunk(p, u, HALF), chunk(p, PER + u), dsend.at[p, u - PER // 2],
            rsem.at[p, PER + u], h0, 2 * (1 - h0) + u % 2,
        )

    def detour(t):
        for p in moved:
            @pl.when((xl == 1 - h0) & (t < PER - FAR))
            def _():
                arrived(tb.at[p, t], far.at[p, t])

                @pl.when(r == 1 - h0)
                def _():
                    transit(p, t)[0].start()

                @pl.when(r == h0)
                def _():
                    transit(p, t)[1].start()

            @pl.when((xl == h0) & (t >= FAR))
            def _():
                @pl.when(r == h0)
                def _():
                    arrived(tb.at[p, t - FAR], far.at[p, t - FAR])
                    transit(p, t - FAR)[2].start()

                @pl.when((r == 1 - h0) & (core == 1))
                def _():
                    for i in range(2):
                        u = 2 * (t - FAR) + PER // 2 + i
                        arrived(chunk(p, u, HALF), bsem.at[p, u])
                        upward(p, u).start()

    @pl.when(swapper)
    def _():
        def early(u):
            swapped(2 * u + core)
            swapped(2 * u + core + PER)
            stage_all(2 * u + core)

            @pl.when(u > 0)
            def _():
                hold_all(u - 1)

        def late(t):
            stage_all(2 * t + core)
            hold_all(t - 1)

        loop(0, PER // 2, early)
        loop(PER // 2, PER, late)
        hold_all(PER - 1)

        def finish_swap(t):
            swapped(2 * t + 1 - core)

        loop(0, PER, finish_swap)
        loop(0, PER, lambda t: stage_all(2 * t + 1 - core))

    for load in loads[1:]:
        load.wait()

    is_n = (r == h0) & (xl == 1 - h0)
    source = (r == h1) & (xl == h1)
    sink = (r == 1 - h1) & (xl == 1 - h1)
    swing = (r == 1 - h1) & (xl == h1)
    g_at = pl.ds(HALF + NB, NB)
    bc_at = pl.ds(HALF, NB)

    def across(t):
        s = 2 * t + core
        src = chunk(0, s, HALF + NB) if same else chunk(0, s)
        return remote(
            src, chunk(0, s, HALF + NB), gsend.at[t], gsem.at[s], 1 - h1, 2 * (1 - h1) + core
        )

    def pick_own():
        if same:
            b[0, g_at, :] = choose(b[0, :NB, :], b[0, NB:HALF, :], odd[1])
        else:
            b[0, g_at, :] = b[0, :NB, :]

    if same:
        @pl.when(source)
        def _():
            pick_own()
            loop(0, PER // 2, lambda t: across(t).start())

    def swing_out(u):
        return remote(
            chunk(0, u, HALF), bo.at[aligned(u, CH), :], osend.at[u], osem.at[u], r, mate
        )

    for p in moved:
        @pl.when((r == halves[p]) & (xl == 1 - halves[p]))
        def _():
            b[p, bc_at, :] = choose(ww[core, :NB, :], ww[core, NB:, :], odd[p]).T

    if not same:
        @pl.when(is_n)
        def _():
            loop(0, PER, lambda u: swing_out(u).start())

    left = pl.ds(0, NB)
    right = pl.ds(NB, NB)
    place = order[...] - r * HALF

    def permutation(i):
        at = lax.broadcasted_iota(jnp.int32, (128, HALF), 0) + i * 128
        pm[aligned(i, 128), :] = jnp.where(at == place, 1.0, 0.0).astype(BF16)

    loop(0, HALF // 128, permutation)

    mixed_rows = lat * steps
    depth = lat * steps * local_vars
    total_vars = lat * local_vars
    pick_latent = (
        lax.broadcasted_iota(jnp.int32, (mixed_rows, lat), 0) // steps
        == lax.broadcasted_iota(jnp.int32, (mixed_rows, lat), 1)
    )
    pick_latent = jnp.where(pick_latent, 1.0, 0.0).astype(BF16)
    along = lax.broadcasted_iota(jnp.int32, (total_vars, depth), 1)
    pick_var = (along // (steps * local_vars)) * local_vars + along % local_vars
    pick_var = pick_var == lax.broadcasted_iota(jnp.int32, (total_vars, depth), 0)
    pick_var = jnp.where(pick_var, 1.0, 0.0).astype(BF16)
    wide = lax.broadcasted_iota(jnp.int32, (mixed_rows, depth), 1)
    tall = lax.broadcasted_iota(jnp.int32, (mixed_rows, depth), 0)
    same_step = (wide // local_vars) % steps == tall % steps

    def mixer(part):
        spread = nn(nn(pick_latent, part).astype(BF16), pick_var)
        return jnp.where(same_step, spread, 0.0).astype(BF16)

    rot_high, rot_low = split(rot[...])
    mix_high, mix_low = mixer(rot_high), mixer(rot_low)

    def to_mate(p, t):
        s = 2 * t + core
        return remote(chunk(p, s), chunk(p, s), pair.at[p, t], rsem.at[p, s], r, mate)

    def to_down(p, t):
        s = 2 * t + core
        return remote(
            chunk(p, s), chunk(p, s % PER, HALF), down.at[p, t], bsem.at[p, s % PER],
            1 - halves[p], 2 * halves[p] + s // PER,
        )

    def product(rows, p):
        near = nt(rows[:, : NB // 2], inv[p, : NB // 2, : NB // 2])
        far = nt(rows, inv[p, NB // 2 :, :])
        return near.astype(BF16), far.astype(BF16)

    def take_step(t):
        @pl.when(xl == 1 - h0)
        def _():
            s = 2 * t + 1 - core
            arrived(chunk(0, s), rsem.at[0, s])

        @pl.when(t % 2 == 1)
        def _():
            at = aligned(t // 2, 4 * CH)
            near, far = product(b[0, at, :], 0)
            fs[at, : NB // 2] = near
            fs[at, NB // 2 :] = far

    def relay(t):
        pass_on(t)
        if same:
            detour(t)

        @pl.when(t > 0)
        def _():
            take_step(t - 1)

    def pass_on(t):
        s = 2 * t + core
        for p in moved:
            @pl.when(xl == 1 - halves[p])
            def _():
                arrived(chunk(p, s), rsem.at[p, s])
                to_mate(p, t).start()

                @pl.when((r == halves[p]) & (t < FAR) if same else r == halves[p])
                def _():
                    to_down(p, t).start()

                if p == 0 and not same:
                    @pl.when((r == h1) & (t < PER // 2))
                    def _():
                        across(t).start()

    loop(0, 2, relay)
    loop(1, lat, lambda d: first(d).wait_recv())
    for i in range(lat):
        for t in range(steps):
            xf[pl.ds((i * steps + t) * local_vars, local_vars), :] = x[i, t].astype(F32)
    samples = xf[...].astype(BF16)
    mixed = nn(mix_high, samples) + nn(mix_low, samples)
    for i in range(lat):
        y[i] = mixed[i * steps : (i + 1) * steps]
    loop(1, lat, lambda d: second(d).start())
    own_z = pltpu.make_async_copy(y.at[lid], z.at[lid], lsem.at[5])
    own_z.start()
    loop(2, 5, relay)
    own_z.wait()
    loop(1, lat, lambda d: second(d).wait_recv())
    for i in range(lat):
        zf[pl.ds(i * steps, steps), :] = z[i]
    high, low = split(zf[...])
    field[...] = nn(high, pm[...]) + nn(low, pm[...])

    def solve(p):
        part = choose(field[:, :NB], field[:, NB:], odd[p])
        if p == 1:
            part = part - nt(solved[0], f[g_at, left])
        top, rest = split(part)
        solved[p] = (nt(top, inv[p]) + nt(rest, inv[p])).astype(BF16)

    def sharing(p):
        return remote(solved.at[p], solved.at[p], vsend.at[p], vsem.at[p], 1 - halves[p], c)

    def share(p):
        @pl.when(r == halves[p])
        def _():
            solve(p)
            sharing(p).start()

    def receive(p):
        @pl.when(r != halves[p])
        def _():
            arrived(solved.at[p], vsem.at[p])

    share(0)
    loop(5, PER, relay)
    take_step(PER - 1)

    if not equal:
        @pl.when(xl == 1 - h1)
        def _():
            def other(t):
                s = 2 * t + 1 - core
                arrived(chunk(1, s), rsem.at[1, s])

            loop(0, PER, other)

    for p in moved:
        @pl.when(r == xl)
        def _():
            own = b[p, aligned(core, NB), :]
            if p == 0 and not same:
                own = choose(own, b[p, aligned(1 - core, NB), :], turned)
            b[p, bc_at, :] = own

        @pl.when((r == 1 - halves[p]) & (xl == halves[p]))
        def _():
            def below(u):
                if same:
                    @pl.when((core == 0) | (u < PER // 2))
                    def _():
                        arrived(chunk(p, u, HALF), bsem.at[p, u])
                else:
                    arrived(chunk(p, u, HALF), bsem.at[p, u])
                if p == 0 and same:
                    swing_out(u).start()

            loop(0, PER, below)

    if not same:
        @pl.when(r == h1)
        def _():
            pick_own()
    else:
        @pl.when((r == h1) & (xl == 1 - h1))
        def _():
            pick_own()

    def sink_pass(t):
        s = 2 * t + core
        return remote(
            chunk(0, s, HALF + NB), chunk(0, s, HALF + NB), gpass.at[t], gsem.at[s], r, mate
        )

    @pl.when(sink)
    def _():
        def take(t):
            s = 2 * t + core
            arrived(chunk(0, s, HALF + NB), gsem.at[s])
            sink_pass(t).start()

        def rest(t):
            s = 2 * t + 1 - core
            arrived(chunk(0, s, HALF + NB), gsem.at[s])

        loop(0, PER // 2, take)
        loop(0, PER // 2, rest)

    @pl.when(swing)
    def _():
        def gather(u):
            arrived(bo.at[aligned(u, CH), :], osem.at[u])

        loop(0, PER, gather)
        even_core = jnp.where(core == 0, 1.0, 0.0)
        b[0, g_at, :] = choose(
            b[0, bc_at, :], bo[...], even_core * odd[1] + (1 - even_core) * (1 - odd[1])
        )

    def keep(p, at, pieces):
        f[at, pl.ds(p * NB, NB // 2)] = pieces[0]
        f[at, pl.ds(p * NB + NB // 2, NB // 2)] = pieces[1]

    def first_factor(i):
        at = aligned(i, TILE)
        keep(0, at, product(b[0, at, :], 0))

    loop(HALF // TILE, 2 * HALF // TILE, first_factor)

    def settle(i):
        at = aligned(i, TILE)
        rows = fs[at, :]
        if not same:
            rows = choose(rows, fs[aligned((i + NB // TILE) % (HALF // TILE), TILE), :], turned)
        f[at, left] = rows

    loop(0, HALF // TILE, settle)

    def second_factor(i):
        at = aligned(i, TILE)
        part = b[last, at, :].astype(F32) - nt(f[at, left], f[g_at, left])
        keep(1, at, product(part.astype(BF16), 1))

    receive(0)
    share(1)
    loop(0, 3 * NB // TILE, second_factor)

    mine = pl.ds(pl.multiple_of(c * 128, 128), 128)
    mine_after = pl.ds(pl.multiple_of(c * 128 + NB, 128), 128)

    def finish(m):
        at = aligned(m, TILE)
        trail[0, at, :] = ww[core, at, :].astype(F32) - nt(f[at, :], f[bc_at, :])
        pans[0, 0, at, :] = f[at, mine]
        pans[0, 1, at, :] = f[at, mine_after]

    loop(0, HALF // TILE, finish)
    receive(1)

    def whiten(m):
        at = aligned(m, TILE)
        white[0, :, at] = field[:, at] - (
            nt(solved[0], f[at, left]) + nt(solved[1], f[at, right])
        )

    loop(0, HALF // TILE, whiten)

    @pl.when(swapper)
    def _():
        loop(0, 2 * PER, lambda s: swapping(s).wait_send())

    for p in moved:
        @pl.when(xl == halves[p])
        def _():
            loop(0, FAR if same else PER, lambda t: holding(p, t).wait_send())
            if same:
                loop(0, PER - FAR, lambda k: holding_far(p, k).wait_send())

        @pl.when(xl == 1 - halves[p])
        def _():
            loop(0, PER, lambda t: to_mate(p, t).wait_send())

            @pl.when(r == halves[p])
            def _():
                loop(0, FAR if same else PER, lambda t: to_down(p, t).wait_send())

        if same:
            @pl.when((xl == 1 - h0) | (r == h0))
            def _():
                loop(0, PER - FAR, lambda k: transit(p, k)[1].wait_send())

            @pl.when((xl == h0) & (r == 1 - h0) & (core == 1))
            def _():
                loop(PER // 2, PER, lambda u: upward(p, u).wait_send())

    for p in range(2):
        @pl.when(r == halves[p])
        def _():
            sharing(p).wait_send()

    @pl.when(source)
    def _():
        loop(0, PER // 2, lambda t: across(t).wait_send())

    @pl.when(sink)
    def _():
        loop(0, PER // 2, lambda t: sink_pass(t).wait_send())

    @pl.when(swing)
    def _():
        loop(0, PER, lambda u: swing_out(u).wait_send())

    loop(1, lat, lambda d: first(d).wait_send())
    loop(1, lat, lambda d: second(d).wait_send())


def solution(mesh):
    lat = mesh.shape["latent"]

    def local(observations, rotation, ordering, working, factor_inverse, panel_index):
        times, local_vars, stations = observations.shape
        steps = times // lat
        vmem = pl.BlockSpec(memory_space=pltpu.VMEM)
        anyw = pl.BlockSpec(memory_space=pl.ANY)
        dma = pltpu.SemaphoreType.DMA

        def call(halves, equal, *operands):
            return pl.pallas_call(
                functools.partial(kernel, halves, equal, lat),
                out_shape=(
                    jax.ShapeDtypeStruct((1, HALF, NB), F32),
                    jax.ShapeDtypeStruct((1, 2, HALF, 128), BF16),
                    jax.ShapeDtypeStruct((1, times, HALF), F32),
                ),
                in_specs=[pl.BlockSpec(memory_space=pltpu.SMEM)] + [anyw] * 5,
                out_specs=(vmem, vmem, vmem),
                scratch_shapes=[
                    pltpu.VMEM((2, NB, NB), BF16),
                    pltpu.VMEM((2, HALF, NB), BF16),
                    pltpu.VMEM((2, 2 * HALF, NB), BF16),
                    pltpu.VMEM((NB, NB), BF16),
                    pltpu.VMEM((2, PER - FAR, CH, NB), BF16),
                    pltpu.VMEM((2 * HALF, 2 * NB), BF16),
                    pltpu.VMEM((HALF, NB), BF16),
                    pltpu.VMEM((lat, steps, local_vars, HALF), BF16),
                    pltpu.VMEM((times * local_vars, HALF), F32),
                    pltpu.VMEM((lat, steps, HALF), F32),
                    pltpu.VMEM((lat, steps, HALF), F32),
                    pltpu.VMEM((times, HALF), F32),
                    pltpu.VMEM((HALF, HALF), BF16),
                    pltpu.VMEM((times, HALF), F32),
                    pltpu.VMEM((2, times, NB), BF16),
                    pltpu.VMEM(rotation.shape[::-1], F32),
                    pltpu.VMEM((1, HALF), jnp.int32),
                    dma((6,)),
                    dma((2, 2 * PER)),
                    dma((2, 2 * PER)),
                    dma((2, PER)),
                    dma((PER,)),
                    dma((PER,)),
                    dma((2,)),
                    dma((2, PER)),
                    dma((2, PER)),
                    dma((2, PER)),
                    dma((PER,)),
                    dma((PER // 2,)),
                    dma((PER // 2,)),
                    dma((2,)),
                    dma((2, PER - FAR)),
                    dma((2, PER - FAR)),
                    dma((2, PER // 2)),
                    dma((lat,)),
                    dma((lat,)),
                    dma((lat,)),
                    dma((lat,)),
                ],
                compiler_params=pltpu.CompilerParams(
                    collective_id=4 + halves[0] if equal else halves[0] * 2 + halves[1], has_side_effects=True,
                    vmem_limit_bytes=48 << 20,
                ),
                name=f"panels_{halves[0]}{halves[1]}{int(equal)}",
            )(*operands)

        branches = [functools.partial(call, (i, j), False) for i in range(2) for j in range(2)]
        branches += [functools.partial(call, (i, i), True) for i in range(2)]
        code = jnp.sum(panel_index * jnp.array([4, 1], jnp.int32))
        upper, lower = code >> 3, (code >> 1) & 1
        choice = jnp.where(lax.rem(code, 5) == 0, 4 + upper, upper * 2 + lower)
        return lax.switch(
            choice, branches,
            panel_index, observations, rotation.T, ordering.reshape(1, HALF), working,
            factor_inverse,
        )

    return jax.shard_map(
        local,
        mesh=mesh,
        in_specs=(
            P("col", "latent", "row"),
            P(),
            P("row"),
            P("latent", "row", "col"),
            P("latent", None, None, None),
            P(),
        ),
        out_specs=(
            P("latent", "row", "col"),
            P("latent", None, "row", "col"),
            P("latent", "col", "row"),
        ),
        check_vma=False,
    )
```

```python
import functools

import jax
import jax.numpy as jnp
from jax import lax
from jax.experimental import pallas as pl
from jax.experimental.pallas import tpu as pltpu
from jax.sharding import PartitionSpec as P

MESH = pl.DeviceIdType.MESH
F32 = jnp.float32
BF16 = jnp.bfloat16
NB = 512
HALF = 1024
PER = 8
CH = NB // PER
TILE = 512
FAR = PER - 2


def nt(a, b):
    return lax.dot_general(a, b, (((1,), (1,)), ((), ())), preferred_element_type=F32)


def nn(a, b):
    return jnp.dot(a, b, preferred_element_type=F32)


def split(value):
    high = value.astype(BF16)
    return high, (value - high.astype(F32)).astype(BF16)


def aligned(index, unit):
    return pl.ds(pl.multiple_of(index * unit, unit), unit)


def loop(start, stop, action):
    def step(i, carry):
        action(i)
        return carry

    lax.fori_loop(start, stop, step, 0)


def kernel(
    halves, equal, lat,
    which, obs, rot_hbm, order_hbm, w_hbm, inv_hbm,
    trail, pans, white,
    inv, ww, b, bo, tb, f, fs, x, xf, y, z, zf, pm, field, solved, rot, order,
    lsem, swap, rsem, bsem, osem, gsem, vsem, hold, pair, down, osend, gsend, gpass, vsend, far, fsend, dsend,
    s1, r1, s2, r2,
):
    h0, h1 = halves
    same = h0 == h1
    moved = (0,) if equal else (0, 1)
    last = moved[-1]
    lid = lax.axis_index("latent")
    r = lax.axis_index("row")
    c = lax.axis_index("col")
    xl = c // 2
    core = c % 2
    mate = 2 * xl + 1 - core
    odd = [(which[p] & 1).astype(F32) for p in range(2)]
    steps = obs.shape[0] // lat
    local_vars = obs.shape[1]
    turned = jnp.where(r == h1, 1.0, 0.0) * odd[1]

    def choose(low, high, weight):
        mix = jnp.full(low.shape, weight, F32).astype(low.dtype)
        return low * (1 - mix) + high * mix

    def remote(src, dst, send, recv, row, col):
        return pltpu.make_async_remote_copy(
            src_ref=src, dst_ref=dst, send_sem=send, recv_sem=recv,
            device_id={"row": row, "col": col}, device_id_type=MESH,
        )

    def arrived(ref, sem):
        pltpu.make_async_copy(ref, ref, sem).wait()

    def chunk(p, s, base=0):
        return b.at[p, pl.ds(pl.multiple_of(base + s * CH, CH), CH), :]

    loads = [
        pltpu.make_async_copy(w_hbm.at[0], ww.at[core], lsem.at[0]),
        pltpu.make_async_copy(inv_hbm.at[0], inv, lsem.at[1]),
        pltpu.make_async_copy(obs.at[pl.ds(lid * steps, steps)], x.at[lid], lsem.at[2]),
        pltpu.make_async_copy(rot_hbm, rot, lsem.at[3]),
        pltpu.make_async_copy(order_hbm, order, lsem.at[4]),
    ]
    loads[0].start()
    for load in loads[1:]:
        load.start()

    barrier = pltpu.get_barrier_semaphore()

    def greet(d):
        pl.semaphore_signal(
            barrier, inc=1, device_id={"latent": lax.rem(lid + d, lat)}, device_id_type=MESH
        )

    def greet_group(d):
        other = lax.rem(r * 4 + c + d, 8)
        pl.semaphore_signal(
            barrier, inc=1, device_id={"row": other // 4, "col": other % 4}, device_id_type=MESH
        )

    loop(1, lat, greet)
    loop(1, 8, greet_group)
    pl.semaphore_wait(barrier, lat - 1 + 7)

    swapper = (xl == h0) | (xl == h1)

    def swapping(s):
        at = aligned(s, CH)
        return remote(
            w_hbm.at[0, at, :], ww.at[core, at, :], swap.at[0, s], swap.at[1, s], r, mate
        )

    def swapped(s):
        arrived(ww.at[1 - core, aligned(s, CH), :], swap.at[1, s])

    @pl.when(swapper)
    def _():
        def needed(u):
            swapping(2 * u + 1 - core).start()
            swapping(2 * u + 1 - core + PER).start()

        def others(u):
            swapping(2 * u + core).start()
            swapping(2 * u + core + PER).start()

        loop(0, PER // 2, needed)
        loop(0, PER // 2, others)

    def first(d):
        to = lax.rem(lid + d, lat)
        return pltpu.make_async_remote_copy(
            src_ref=obs.at[pl.ds(to * steps, steps)], dst_ref=x.at[lid],
            send_sem=s1.at[d], recv_sem=r1.at[d],
            device_id={"latent": to}, device_id_type=MESH,
        )

    def second(d):
        to = lax.rem(lid + d, lat)
        return pltpu.make_async_remote_copy(
            src_ref=y.at[to], dst_ref=z.at[lid],
            send_sem=s2.at[d], recv_sem=r2.at[d],
            device_id={"latent": to}, device_id_type=MESH,
        )

    loop(1, lat, lambda d: first(d).start())
    loads[0].wait()

    def holding(p, t):
        s = 2 * t + core
        return remote(chunk(p, s), chunk(p, s), hold.at[p, t], rsem.at[p, s], r, 2 * (1 - xl) + core)

    def stage(p, s):
        at = aligned(s, CH)
        value = choose(ww[0, at, :], ww[1, at, :], odd[p])
        if p == 0 and not same:
            flip = aligned((s + PER) % (2 * PER), CH)
            value = choose(value, choose(ww[0, flip, :], ww[1, flip, :], odd[p]), turned)
        b[p, at, :] = value

    def stage_all(s):
        for p in moved:
            @pl.when(xl == halves[p])
            def _():
                stage(p, s)

    def holding_far(p, k):
        return remote(
            chunk(p, 2 * (FAR + k) + core), tb.at[p, k], hold.at[p, FAR + k], far.at[p, k],
            1 - r, 2 * (1 - xl) + core,
        )

    def hold_all(t):
        for p in moved:
            near = (xl == halves[p]) & (t < FAR) if same else xl == halves[p]

            @pl.when(near)
            def _():
                holding(p, t).start()

            if same:
                @pl.when((xl == h0) & (t >= FAR))
                def _():
                    holding_far(p, t - FAR).start()

    def transit(p, k):
        s = 2 * (FAR + k) + core
        src, sem = tb.at[p, k], fsend.at[p, k]
        to_d = remote(
            src, chunk(p, s - PER, HALF), sem, bsem.at[p, s - PER], 1 - h0, 2 * h0 + 1
        )
        to_s = remote(src, tb.at[p, k], sem, far.at[p, k], h0, 2 * h0 + core)
        to_t = remote(src, chunk(p, s), sem, rsem.at[p, s], 1 - h0, 2 * (1 - h0) + core)
        return to_d, to_s, to_t

    def upward(p, u):
        return remote(
            chunk(p, u, HALF), chunk(p, PER + u), dsend.at[p, u - PER // 2],
            rsem.at[p, PER + u], h0, 2 * (1 - h0) + u % 2,
        )

    def detour(t):
        for p in moved:
            @pl.when((xl == 1 - h0) & (t < PER - FAR))
            def _():
                arrived(tb.at[p, t], far.at[p, t])

                @pl.when(r == 1 - h0)
                def _():
                    transit(p, t)[0].start()

                @pl.when(r == h0)
                def _():
                    transit(p, t)[1].start()

            @pl.when((xl == h0) & (t >= FAR))
            def _():
                @pl.when(r == h0)
                def _():
                    arrived(tb.at[p, t - FAR], far.at[p, t - FAR])
                    transit(p, t - FAR)[2].start()

                @pl.when((r == 1 - h0) & (core == 1))
                def _():
                    for i in range(2):
                        u = 2 * (t - FAR) + PER // 2 + i
                        arrived(chunk(p, u, HALF), bsem.at[p, u])
                        upward(p, u).start()

    @pl.when(swapper)
    def _():
        def early(u):
            swapped(2 * u + core)
            swapped(2 * u + core + PER)
            stage_all(2 * u + core)

            @pl.when(u > 0)
            def _():
                hold_all(u - 1)

        def late(t):
            stage_all(2 * t + core)
            hold_all(t - 1)

        loop(0, PER // 2, early)
        loop(PER // 2, PER, late)
        hold_all(PER - 1)

        def finish_swap(t):
            swapped(2 * t + 1 - core)

        loop(0, PER, finish_swap)
        loop(0, PER, lambda t: stage_all(2 * t + 1 - core))

    for load in loads[1:]:
        load.wait()

    is_n = (r == h0) & (xl == 1 - h0)
    source = (r == h1) & (xl == h1)
    sink = (r == 1 - h1) & (xl == 1 - h1)
    swing = (r == 1 - h1) & (xl == h1)
    g_at = pl.ds(HALF + NB, NB)
    bc_at = pl.ds(HALF, NB)

    def across(t):
        s = 2 * t + core
        src = chunk(0, s, HALF + NB) if same else chunk(0, s)
        return remote(
            src, chunk(0, s, HALF + NB), gsend.at[t], gsem.at[s], 1 - h1, 2 * (1 - h1) + core
        )

    def pick_own():
        if same:
            b[0, g_at, :] = choose(b[0, :NB, :], b[0, NB:HALF, :], odd[1])
        else:
            b[0, g_at, :] = b[0, :NB, :]

    if same:
        @pl.when(source)
        def _():
            pick_own()
            loop(0, PER // 2, lambda t: across(t).start())

    def swing_out(u):
        return remote(
            chunk(0, u, HALF), bo.at[aligned(u, CH), :], osend.at[u], osem.at[u], r, mate
        )

    for p in moved:
        @pl.when((r == halves[p]) & (xl == 1 - halves[p]))
        def _():
            b[p, bc_at, :] = choose(ww[core, :NB, :], ww[core, NB:, :], odd[p]).T

    if not same:
        @pl.when(is_n)
        def _():
            loop(0, PER, lambda u: swing_out(u).start())

    left = pl.ds(0, NB)
    right = pl.ds(NB, NB)
    place = order[...] - r * HALF

    def permutation(i):
        at = lax.broadcasted_iota(jnp.int32, (128, HALF), 0) + i * 128
        pm[aligned(i, 128), :] = jnp.where(at == place, 1.0, 0.0).astype(BF16)

    loop(0, HALF // 128, permutation)

    mixed_rows = lat * steps
    depth = lat * steps * local_vars
    total_vars = lat * local_vars
    pick_latent = (
        lax.broadcasted_iota(jnp.int32, (mixed_rows, lat), 0) // steps
        == lax.broadcasted_iota(jnp.int32, (mixed_rows, lat), 1)
    )
    pick_latent = jnp.where(pick_latent, 1.0, 0.0).astype(BF16)
    along = lax.broadcasted_iota(jnp.int32, (total_vars, depth), 1)
    pick_var = (along // (steps * local_vars)) * local_vars + along % local_vars
    pick_var = pick_var == lax.broadcasted_iota(jnp.int32, (total_vars, depth), 0)
    pick_var = jnp.where(pick_var, 1.0, 0.0).astype(BF16)
    wide = lax.broadcasted_iota(jnp.int32, (mixed_rows, depth), 1)
    tall = lax.broadcasted_iota(jnp.int32, (mixed_rows, depth), 0)
    same_step = (wide // local_vars) % steps == tall % steps

    def mixer(part):
        spread = nn(nn(pick_latent, part).astype(BF16), pick_var)
        return jnp.where(same_step, spread, 0.0).astype(BF16)

    rot_high, rot_low = split(rot[...])
    mix_high, mix_low = mixer(rot_high), mixer(rot_low)

    def to_mate(p, t):
        s = 2 * t + core
        return remote(chunk(p, s), chunk(p, s), pair.at[p, t], rsem.at[p, s], r, mate)

    def to_down(p, t):
        s = 2 * t + core
        return remote(
            chunk(p, s), chunk(p, s % PER, HALF), down.at[p, t], bsem.at[p, s % PER],
            1 - halves[p], 2 * halves[p] + s // PER,
        )

    def product(rows, p):
        near = nt(rows[:, : NB // 2], inv[p, : NB // 2, : NB // 2])
        far = nt(rows, inv[p, NB // 2 :, :])
        return near.astype(BF16), far.astype(BF16)

    def take_step(t):
        @pl.when(xl == 1 - h0)
        def _():
            s = 2 * t + 1 - core
            arrived(chunk(0, s), rsem.at[0, s])

        @pl.when(t % 2 == 1)
        def _():
            at = aligned(t // 2, 4 * CH)
            near, far = product(b[0, at, :], 0)
            fs[at, : NB // 2] = near
            fs[at, NB // 2 :] = far

    def relay(t):
        pass_on(t)
        if same:
            detour(t)

        @pl.when(t > 0)
        def _():
            take_step(t - 1)

    def pass_on(t):
        s = 2 * t + core
        for p in moved:
            @pl.when(xl == 1 - halves[p])
            def _():
                arrived(chunk(p, s), rsem.at[p, s])
                to_mate(p, t).start()

                @pl.when((r == halves[p]) & (t < FAR) if same else r == halves[p])
                def _():
                    to_down(p, t).start()

                if p == 0 and not same:
                    @pl.when((r == h1) & (t < PER // 2))
                    def _():
                        across(t).start()

    loop(0, 2, relay)
    loop(1, lat, lambda d: first(d).wait_recv())
    for i in range(lat):
        for t in range(steps):
            xf[pl.ds((i * steps + t) * local_vars, local_vars), :] = x[i, t].astype(F32)
    samples = xf[...].astype(BF16)
    doubled = nn(jnp.concatenate([mix_high, mix_low], axis=0), samples)
    mixed = doubled[:mixed_rows] + doubled[mixed_rows:]
    for i in range(lat):
        y[i] = mixed[i * steps : (i + 1) * steps]
    loop(1, lat, lambda d: second(d).start())
    own_z = pltpu.make_async_copy(y.at[lid], z.at[lid], lsem.at[5])
    own_z.start()
    loop(2, 5, relay)
    own_z.wait()
    loop(1, lat, lambda d: second(d).wait_recv())
    for i in range(lat):
        zf[pl.ds(i * steps, steps), :] = z[i]
    both = nn(jnp.concatenate(split(zf[...]), axis=0), pm[...])
    field[...] = both[: zf.shape[0]] + both[zf.shape[0] :]

    def solve(p):
        part = choose(field[:, :NB], field[:, NB:], odd[p])
        if p == 1:
            part = part - nt(solved[0], f[g_at, left])
        both = nt(jnp.concatenate(split(part), axis=0), inv[p])
        solved[p] = (both[: part.shape[0]] + both[part.shape[0] :]).astype(BF16)

    def sharing(p):
        return remote(solved.at[p], solved.at[p], vsend.at[p], vsem.at[p], 1 - halves[p], c)

    def share(p):
        @pl.when(r == halves[p])
        def _():
            solve(p)
            sharing(p).start()

    def receive(p):
        @pl.when(r != halves[p])
        def _():
            arrived(solved.at[p], vsem.at[p])

    share(0)
    loop(5, PER, relay)
    take_step(PER - 1)

    if not equal:
        @pl.when(xl == 1 - h1)
        def _():
            def other(t):
                s = 2 * t + 1 - core
                arrived(chunk(1, s), rsem.at[1, s])

            loop(0, PER, other)

    for p in moved:
        @pl.when(r == xl)
        def _():
            own = b[p, aligned(core, NB), :]
            if p == 0 and not same:
                own = choose(own, b[p, aligned(1 - core, NB), :], turned)
            b[p, bc_at, :] = own

        @pl.when((r == 1 - halves[p]) & (xl == halves[p]))
        def _():
            def below(u):
                if same:
                    @pl.when((core == 0) | (u < PER // 2))
                    def _():
                        arrived(chunk(p, u, HALF), bsem.at[p, u])
                else:
                    arrived(chunk(p, u, HALF), bsem.at[p, u])
                if p == 0 and same:
                    swing_out(u).start()

            loop(0, PER, below)

    if not same:
        @pl.when(r == h1)
        def _():
            pick_own()
    else:
        @pl.when((r == h1) & (xl == 1 - h1))
        def _():
            pick_own()

    def sink_pass(t):
        s = 2 * t + core
        return remote(
            chunk(0, s, HALF + NB), chunk(0, s, HALF + NB), gpass.at[t], gsem.at[s], r, mate
        )

    @pl.when(sink)
    def _():
        def take(t):
            s = 2 * t + core
            arrived(chunk(0, s, HALF + NB), gsem.at[s])
            sink_pass(t).start()

        def rest(t):
            s = 2 * t + 1 - core
            arrived(chunk(0, s, HALF + NB), gsem.at[s])

        loop(0, PER // 2, take)
        loop(0, PER // 2, rest)

    @pl.when(swing)
    def _():
        def gather(u):
            arrived(bo.at[aligned(u, CH), :], osem.at[u])

        loop(0, PER, gather)
        even_core = jnp.where(core == 0, 1.0, 0.0)
        b[0, g_at, :] = choose(
            b[0, bc_at, :], bo[...], even_core * odd[1] + (1 - even_core) * (1 - odd[1])
        )

    def keep(p, at, pieces):
        f[at, pl.ds(p * NB, NB // 2)] = pieces[0]
        f[at, pl.ds(p * NB + NB // 2, NB // 2)] = pieces[1]

    def first_factor(i):
        at = aligned(i, TILE)
        keep(0, at, product(b[0, at, :], 0))

    loop(HALF // TILE, 2 * HALF // TILE, first_factor)

    def settle(i):
        at = aligned(i, TILE)
        rows = fs[at, :]
        if not same:
            rows = choose(rows, fs[aligned((i + NB // TILE) % (HALF // TILE), TILE), :], turned)
        f[at, left] = rows

    loop(0, HALF // TILE, settle)

    def second_factor(i):
        at = aligned(i, TILE)
        part = b[last, at, :].astype(F32) - nt(f[at, left], f[g_at, left])
        keep(1, at, product(part.astype(BF16), 1))

    receive(0)
    share(1)
    loop(0, 3 * NB // TILE, second_factor)

    mine = pl.ds(pl.multiple_of(c * 128, 128), 128)
    mine_after = pl.ds(pl.multiple_of(c * 128 + NB, 128), 128)

    def finish(m):
        at = aligned(m, TILE)
        trail[0, at, :] = ww[core, at, :].astype(F32) - nt(f[at, :], f[bc_at, :])
        pans[0, 0, at, :] = f[at, mine]
        pans[0, 1, at, :] = f[at, mine_after]

    loop(0, HALF // TILE, finish)
    receive(1)

    def whiten(m):
        at = aligned(m, TILE)
        white[0, :, at] = field[:, at] - (
            nt(solved[0], f[at, left]) + nt(solved[1], f[at, right])
        )

    loop(0, HALF // TILE, whiten)

    @pl.when(swapper)
    def _():
        loop(0, 2 * PER, lambda s: swapping(s).wait_send())

    for p in moved:
        @pl.when(xl == halves[p])
        def _():
            loop(0, FAR if same else PER, lambda t: holding(p, t).wait_send())
            if same:
                loop(0, PER - FAR, lambda k: holding_far(p, k).wait_send())

        @pl.when(xl == 1 - halves[p])
        def _():
            loop(0, PER, lambda t: to_mate(p, t).wait_send())

            @pl.when(r == halves[p])
            def _():
                loop(0, FAR if same else PER, lambda t: to_down(p, t).wait_send())

        if same:
            @pl.when((xl == 1 - h0) | (r == h0))
            def _():
                loop(0, PER - FAR, lambda k: transit(p, k)[1].wait_send())

            @pl.when((xl == h0) & (r == 1 - h0) & (core == 1))
            def _():
                loop(PER // 2, PER, lambda u: upward(p, u).wait_send())

    for p in range(2):
        @pl.when(r == halves[p])
        def _():
            sharing(p).wait_send()

    @pl.when(source)
    def _():
        loop(0, PER // 2, lambda t: across(t).wait_send())

    @pl.when(sink)
    def _():
        loop(0, PER // 2, lambda t: sink_pass(t).wait_send())

    @pl.when(swing)
    def _():
        loop(0, PER, lambda u: swing_out(u).wait_send())

    loop(1, lat, lambda d: first(d).wait_send())
    loop(1, lat, lambda d: second(d).wait_send())


def solution(mesh):
    lat = mesh.shape["latent"]

    def local(observations, rotation, ordering, working, factor_inverse, panel_index):
        times, local_vars, stations = observations.shape
        steps = times // lat
        vmem = pl.BlockSpec(memory_space=pltpu.VMEM)
        anyw = pl.BlockSpec(memory_space=pl.ANY)
        dma = pltpu.SemaphoreType.DMA

        def call(halves, equal, *operands):
            return pl.pallas_call(
                functools.partial(kernel, halves, equal, lat),
                out_shape=(
                    jax.ShapeDtypeStruct((1, HALF, NB), F32),
                    jax.ShapeDtypeStruct((1, 2, HALF, 128), BF16),
                    jax.ShapeDtypeStruct((1, times, HALF), F32),
                ),
                in_specs=[pl.BlockSpec(memory_space=pltpu.SMEM)] + [anyw] * 5,
                out_specs=(vmem, vmem, vmem),
                scratch_shapes=[
                    pltpu.VMEM((2, NB, NB), BF16),
                    pltpu.VMEM((2, HALF, NB), BF16),
                    pltpu.VMEM((2, 2 * HALF, NB), BF16),
                    pltpu.VMEM((NB, NB), BF16),
                    pltpu.VMEM((2, PER - FAR, CH, NB), BF16),
                    pltpu.VMEM((2 * HALF, 2 * NB), BF16),
                    pltpu.VMEM((HALF, NB), BF16),
                    pltpu.VMEM((lat, steps, local_vars, HALF), BF16),
                    pltpu.VMEM((times * local_vars, HALF), F32),
                    pltpu.VMEM((lat, steps, HALF), F32),
                    pltpu.VMEM((lat, steps, HALF), F32),
                    pltpu.VMEM((times, HALF), F32),
                    pltpu.VMEM((HALF, HALF), BF16),
                    pltpu.VMEM((times, HALF), F32),
                    pltpu.VMEM((2, times, NB), BF16),
                    pltpu.VMEM(rotation.shape[::-1], F32),
                    pltpu.VMEM((1, HALF), jnp.int32),
                    dma((6,)),
                    dma((2, 2 * PER)),
                    dma((2, 2 * PER)),
                    dma((2, PER)),
                    dma((PER,)),
                    dma((PER,)),
                    dma((2,)),
                    dma((2, PER)),
                    dma((2, PER)),
                    dma((2, PER)),
                    dma((PER,)),
                    dma((PER // 2,)),
                    dma((PER // 2,)),
                    dma((2,)),
                    dma((2, PER - FAR)),
                    dma((2, PER - FAR)),
                    dma((2, PER // 2)),
                    dma((lat,)),
                    dma((lat,)),
                    dma((lat,)),
                    dma((lat,)),
                ],
                compiler_params=pltpu.CompilerParams(
                    collective_id=4 + halves[0] if equal else halves[0] * 2 + halves[1], has_side_effects=True,
                    vmem_limit_bytes=48 << 20,
                ),
                name=f"panels_{halves[0]}{halves[1]}{int(equal)}",
            )(*operands)

        kinds = [
            ((0, 1), False), ((1, 0), False), ((0, 0), False), ((1, 1), False),
            ((0, 0), True), ((1, 1), True),
        ]
        branches = [functools.partial(call, *kind) for kind in kinds]
        table = sum(kind << (3 * n) for n, kind in enumerate((1, 1, 1, 2, 4, 2, 3, 5, 3)))
        half, parity = panel_index >> 1, panel_index & 1
        place = jnp.sum(
            half * jnp.array([-9, 18], jnp.int32) + parity * jnp.array([3, -3], jnp.int32) + 6
        )
        choice = (jnp.int32(table) >> jnp.minimum(place, 31)) & 7
        return lax.switch(
            choice, branches,
            panel_index, observations, rotation.T, ordering.reshape(1, HALF), working,
            factor_inverse,
        )

    return jax.shard_map(
        local,
        mesh=mesh,
        in_specs=(
            P("col", "latent", "row"),
            P(),
            P("row"),
            P("latent", "row", "col"),
            P("latent", None, None, None),
            P(),
        ),
        out_specs=(
            P("latent", "row", "col"),
            P("latent", None, "row", "col"),
            P("latent", "col", "row"),
        ),
        check_vma=False,
    )
```
